32 devices in a mesh: grp: 4 (over y, x), own: 8 (over z, core).
Axes of the slice: x: 2, y: 2, z: 4, core: 2. Of those that a mesh axis runs over, the one named last changes fastest.
Arguments:
- embeddings: float32 [24576, 768], P(('grp', 'own')), may hold values from -64 to 64
- cluster_ids: int32 [24576], P(('grp', 'own')), may hold values from 0 to 127, as said below
- owner_map: int32 [128], replicated, may hold values from 0 to 7, as said below
- source_order: int32 [24576], P(('grp', 'own')), may hold values from 0 to 767, as said below
Outputs:
- dup_score: float32 [24576], P(('grp', 'own'))
- centroids: float32 [128, 768], P('own')
The draws below stay inside these ranges and needn't reach their ends.
Inputs may be any that keep to these rules, and one draw needn't show every extreme that they name: `owner_map`: every owner index is given to exactly 16 clusters. `cluster_ids`: within the 768 rows of one device, at most 192 rows have clusters of one owner index; in every draw some owner index receives exactly 192 rows from every device, and every device sends exactly 192 rows to some owner index. Cluster sizes are uneven and some clusters may be empty. `source_order`: each aligned block of 768 entries is a permutation of 0 to 767.
All inputs are finite; a program needn't handle non-finite values.
Results may differ from the reference program's by a relative error of at most 0.0003.
Values sent between devices are 32-bit elements; how exact they have to be, the bound alone decides.
No kernel may reach another device: no remote copies, remote signals or barrier semaphores. Data moves between devices by JAX's collectives and lax.ppermute only.
A program may use at most 128 MiB of HBM per device.

```python
import jax
import jax.numpy as jnp
from jax import lax

D = 768
R_DEV = 768
CL_OWN = 16
CLUSTERS = 128
CAP = 192
ROWS = 24576
N_GRP = 4
N_OWN = 8


def layout(base_key):
    owner_total = CLUSTERS // CL_OWN
    block_total = ROWS // R_DEV
    slot_total = owner_total * CAP
    cluster_perm = jax.random.permutation(jax.random.fold_in(base_key, 11), CLUSTERS).astype(jnp.int32)
    owner_map = (cluster_perm // CL_OWN).astype(jnp.int32)
    owned_cluster = jnp.argsort(cluster_perm).astype(jnp.int32)
    hot_owner = jax.random.randint(jax.random.fold_in(base_key, 12), (), 0, owner_total)
    base_bias = jax.random.randint(jax.random.fold_in(base_key, 13), (owner_total,), 0, 4)
    owner_index = jnp.arange(owner_total, dtype=jnp.int32)
    slot_owner = jnp.arange(slot_total, dtype=jnp.int32) // CAP

    def one_block(block_key):
        forced = jax.random.randint(jax.random.fold_in(block_key, 1), (), 0, owner_total)
        extra_bias = jax.random.randint(jax.random.fold_in(block_key, 2), (owner_total,), 0, 2)
        owner_bias = jnp.where(owner_index == forced, -2, base_bias + extra_bias)
        owner_bias = jnp.where(owner_index == hot_owner, -3, owner_bias)
        slot_perm = jax.random.permutation(jax.random.fold_in(block_key, 3), slot_total).astype(jnp.int32)
        slot_score = owner_bias[slot_owner] * slot_total + slot_perm
        chosen = jnp.argsort(slot_score)[:R_DEV]
        row_perm = jax.random.permutation(jax.random.fold_in(block_key, 4), R_DEV)
        row_owner = slot_owner[chosen][row_perm]
        upper_bound = jax.random.randint(jax.random.fold_in(block_key, 5), (R_DEV,), 1, CL_OWN + 1)
        local_index = jax.random.randint(jax.random.fold_in(block_key, 6), (R_DEV,), 0, upper_bound)
        return owned_cluster[row_owner * CL_OWN + local_index]
    block_keys = jax.random.split(jax.random.fold_in(base_key, 14), block_total)
    cluster_ids = lax.map(one_block, block_keys).reshape(ROWS).astype(jnp.int32)
    return (owner_map, cluster_ids)


def draw_owner_map(key, part):
    return layout(key)[0]


def draw_cluster_ids(key, part):
    return layout(key)[1]


def draw_embeddings(key, part):
    owner_map, cluster_ids = layout(key)
    direction_count = 16
    base_count = 8
    centers = jnp.clip(jax.random.normal(jax.random.fold_in(key, 21), (CLUSTERS, D), jnp.float32), -4.0, 4.0)
    directions = jnp.clip(jax.random.normal(jax.random.fold_in(key, 25), (CLUSTERS, direction_count, D), jnp.float32), -4.0, 4.0)
    pick_first = jax.random.randint(jax.random.fold_in(key, 26), (ROWS,), 0, direction_count)
    pick_second = jax.random.randint(jax.random.fold_in(key, 27), (ROWS,), 0, direction_count)
    mix_weights = jax.random.uniform(jax.random.fold_in(key, 28), (ROWS, 2), jnp.float32, 0.3, 1.5)
    sub_part = mix_weights[:, 0:1] * directions[cluster_ids, pick_first] + mix_weights[:, 1:2] * directions[cluster_ids, pick_second]
    strength = jnp.exp(jax.random.uniform(jax.random.fold_in(key, 23), (ROWS, 1), jnp.float32, jnp.log(0.3), jnp.log(3.0)))
    copy_bases = jnp.clip(jax.random.normal(jax.random.fold_in(key, 29), (CLUSTERS, base_count, D), jnp.float32), -4.0, 4.0)
    copy_pick = jax.random.randint(jax.random.fold_in(key, 30), (ROWS,), 0, base_count)
    copy_flag = jax.random.uniform(jax.random.fold_in(key, 31), (ROWS, 1), jnp.float32) < 0.15
    jitter_level = jax.random.uniform(jax.random.fold_in(key, 32), (ROWS, 1), jnp.float32, 0.1, 0.33)
    noise_part = jnp.clip(jax.random.normal(jax.random.fold_in(key, 22), (ROWS, D), jnp.float32), -4.0, 4.0)
    main_row = strength * centers[cluster_ids] + sub_part + noise_part
    copy_row = centers[cluster_ids] + copy_bases[cluster_ids, copy_pick] + 1.41421356 * jitter_level * noise_part
    chosen_row = jnp.where(copy_flag, copy_row, main_row)
    return jnp.clip(chosen_row, -64.0, 64.0)


def block_order(block_key):
    return jax.random.permutation(block_key, R_DEV).astype(jnp.int32)


def draw_source_order(key, part):
    block_keys = jax.random.split(jax.random.fold_in(key, 31), ROWS // R_DEV)
    return lax.map(block_order, block_keys).reshape(ROWS)


def setup_inputs(seed: int = 0) -> dict:
    key_list = jax.random.split(jax.random.key(seed), 5)
    embeddings = draw_embeddings(jax.random.fold_in(key_list[4], 71), 0)
    cluster_ids = draw_cluster_ids(jax.random.fold_in(key_list[4], 71), 0)
    owner_map = draw_owner_map(jax.random.fold_in(key_list[4], 71), 0)
    source_order = draw_source_order(jax.random.fold_in(key_list[4], 71), 0)
    return {"embeddings": embeddings, "cluster_ids": cluster_ids, "owner_map": owner_map, "source_order": source_order}


sharpness = 6.0

def unit_rows(embeddings):
    squares = lax.optimization_barrier(jnp.sum(embeddings * embeddings, axis=1, keepdims=True))
    return embeddings * lax.rsqrt(squares + 1e-06)

def owner_positions(owner_map):
    cluster_index = jnp.arange(owner_map.shape[0], dtype=jnp.int32)
    same_owner = owner_map[:, None] == owner_map[None, :]
    earlier = cluster_index[None, :] < cluster_index[:, None]
    before = lax.optimization_barrier(jnp.sum((same_owner & earlier).astype(jnp.int32), axis=1)).astype(jnp.int32)
    return (owner_map * CL_OWN + before).astype(jnp.int32)

def owner_mass(owner_pair):
    owner_rows, owner_ids = owner_pair
    pool_count = owner_rows.shape[0]
    block_rows = 512 if pool_count % 512 == 0 else pool_count
    right_rows = owner_rows
    left_blocks = right_rows.reshape(pool_count // block_rows, block_rows, right_rows.shape[1])
    left_ids = owner_ids.reshape(pool_count // block_rows, block_rows)

    def one_block(block_pair):
        scores = jnp.dot(block_pair[0], right_rows.T, precision=lax.Precision.HIGHEST)
        linked = (block_pair[1][:, None] == owner_ids[None, :]) & (block_pair[1][:, None] >= 0)
        return lax.optimization_barrier(jnp.sum(jnp.where(linked, jnp.exp(sharpness * (scores - 1.0)), 0.0), axis=1))
    return lax.map(one_block, (left_blocks, left_ids)).reshape(pool_count)

def reference(embeddings, cluster_ids, owner_map, source_order):
    device_total = N_GRP * N_OWN
    unit_embed = unit_rows(embeddings)
    row_owner = owner_map[cluster_ids].astype(jnp.int32)
    owner_hot = (row_owner.reshape(device_total, R_DEV)[:, :, None] == jnp.arange(N_OWN, dtype=jnp.int32)[None, None, :]).astype(jnp.int32)
    rank_index = (lax.optimization_barrier(jnp.sum(jnp.cumsum(owner_hot, axis=1) * owner_hot, axis=2)) - 1).reshape(ROWS).astype(jnp.int32)
    source_index = (jnp.arange(ROWS, dtype=jnp.int32) // R_DEV).astype(jnp.int32)
    column_index = (source_index * CAP + rank_index).astype(jnp.int32)
    pool_count = device_total * CAP
    owner_rows = jnp.zeros((N_OWN, pool_count, D), unit_embed.dtype).at[row_owner, column_index].set(unit_embed)
    owner_ids = jnp.full((N_OWN, pool_count), -1, jnp.int32).at[row_owner, column_index].set(cluster_ids)
    dup_mass = lax.map(owner_mass, (owner_rows, owner_ids))
    row_score = jnp.log(dup_mass[row_owner, column_index])
    target_index = (source_index * R_DEV + source_order).astype(jnp.int32)
    dup_score = jnp.zeros((ROWS,), jnp.float32).at[target_index].set(row_score)
    position = owner_positions(owner_map)
    cluster_sums = jax.ops.segment_sum(unit_embed, position[cluster_ids], num_segments=CLUSTERS)
    centroids = cluster_sums * lax.rsqrt(lax.optimization_barrier(jnp.mean(cluster_sums * cluster_sums, axis=1, keepdims=True)) + 1e-06)
    return (dup_score, centroids)
```

```python
import functools

import jax
import jax.numpy as jnp
from jax import lax
from jax.experimental import pallas as pl
from jax.experimental.pallas import tpu as pltpu
from jax.sharding import Mesh
from jax.sharding import PartitionSpec as P


SHARPNESS = 6.0
CHUNKS = 3
TILES = 2
LANES = 128
VMEM = pltpu.VMEM
EVERY = ("grp", "outer", "inner")
PLANE = ("grp", "inner")
LINE = ("outer", "inner")
BY_LEVEL = ("outer", "grp", "inner")
NT = (((1,), (1,)), ((), ()))


def iota(shape, axis):
    return lax.broadcasted_iota(jnp.int32, shape, axis)


def mm(left, right):
    return jnp.dot(left, right, preferred_element_type=jnp.float32)


def mm_nt(left, right):
    return lax.dot_general(left, right, NT, preferred_element_type=jnp.float32)


def halves(value):
    high = value.astype(jnp.bfloat16)
    low = (value - high.astype(jnp.float32)).astype(jnp.bfloat16)
    return high, low


def hot(mask):
    return jnp.where(mask, 1.0, 0.0).astype(jnp.bfloat16)


def cost(micros):
    return pl.CostEstimate(flops=int(micros * 1.1e9), transcendentals=0, bytes_accessed=0)


def call(body, outs, *args, micros, scratch=(), smem=0, aliases=None):
    spec = [pl.BlockSpec(memory_space=pltpu.SMEM)] * smem
    spec += [pl.BlockSpec(memory_space=VMEM)] * (len(args) - smem)
    return pl.pallas_call(
        body,
        out_shape=outs,
        in_specs=spec,
        out_specs=jax.tree.map(lambda _: pl.BlockSpec(memory_space=VMEM), outs),
        scratch_shapes=list(scratch),
        input_output_aliases=aliases or {},
        cost_estimate=cost(micros),
    )(*args)


def out(shape, dtype=jnp.float32):
    return jax.ShapeDtypeStruct(shape, dtype)


def chunk_rows(owner, rank, high, low, k, owners, per):
    inside = (rank >= k * per) & (rank < (k + 1) * per)
    dest = jnp.where(inside, owner * per + rank - k * per, -1)
    pick = hot(iota((owners * per, dest.shape[1]), 0) == dest)
    return mm(pick, high) + mm(pick, low)


def front_body(owners, per, x_ref, ids_ref, om_ref, omr_ref, chunk_ref, high_ref, low_ref, info_ref, sid_ref):
    x = x_ref[...]
    ids = ids_ref[...]
    om = om_ref[...]
    rows = x.shape[0]
    clusters = om.shape[0]
    cap = sid_ref.shape[1]
    square = (clusters, clusters)
    here = iota((clusters, rows), 0) == ids
    owner = jnp.sum(jnp.where(here, om, 0), axis=0, keepdims=True)
    mine = iota((owners, rows), 0) == owner
    member = hot(here)
    within = mm(member, hot(iota((rows, rows), 0) < iota((rows, rows), 1)))
    earlier = hot((om == omr_ref[...]) & (iota(square, 1) < iota(square, 0)))
    base = jnp.sum(mm(earlier, member), axis=1, keepdims=True)
    rank = jnp.sum(jnp.where(here, within + base, 0.0), axis=0, keepdims=True)
    count = jnp.sum(mine.astype(jnp.float32), axis=1, keepdims=True)
    count = jnp.sum(jnp.where(mine, count, 0.0), axis=0, keepdims=True)
    rank = jnp.floor((rank * cap + 0.5) / count).astype(jnp.int32)
    info_ref[...] = jnp.concatenate([owner, rank] * 4, axis=0)
    unit = x * lax.rsqrt(jnp.sum(x * x, axis=1, keepdims=True) + 1e-6)
    high, low = halves(unit)
    high_ref[...] = high
    low_ref[...] = low
    chunk_ref[...] = chunk_rows(owner, rank, high, low, 0, owners, per)
    at_rank = hot(iota((cap, rows), 0) == rank)
    coarse = (ids + 1) // 16
    fine = ids + 1 - coarse * 16
    coarse = jnp.where(mine, coarse.astype(jnp.float32), 0.0).astype(jnp.bfloat16)
    fine = jnp.where(mine, fine.astype(jnp.float32), 0.0).astype(jnp.bfloat16)
    sid = mm_nt(coarse, at_rank) * 16.0 + mm_nt(fine, at_rank)
    sid_ref[...] = sid.astype(jnp.int32) - 1


def back_body(owners, per, chunks, held, high_ref, low_ref, info_ref, ids_ref, om_ref, omr_ref, so_ref, *outs):
    high = high_ref[...]
    low = low_ref[...]
    owner = info_ref[0:1, :]
    rank = info_ref[1:2, :]
    rows = high.shape[0]
    clusters = om_ref.shape[0]
    for k in range(1, chunks):
        outs[k - 1][...] = chunk_rows(owner, rank, high, low, k, owners, per)
    sums_ref, q_ref = outs[chunks - 1 :]
    om = om_ref[...]
    square = (clusters, clusters)
    earlier = (om == omr_ref[...]) & (iota(square, 1) < iota(square, 0))
    position = om * held + jnp.sum(earlier.astype(jnp.int32), axis=1, keepdims=True)
    here = iota((clusters, rows), 0) == ids_ref[...]
    row_position = jnp.sum(jnp.where(here, position, 0), axis=0, keepdims=True)
    pick = hot(iota((clusters, rows), 0) == row_position)
    sums_ref[...] = mm(pick, high) + mm(pick, low)
    target = hot(iota((rows, rows), 0) == so_ref[...])
    values = info_ref[...].astype(jnp.float32).astype(jnp.bfloat16)
    q_ref[...] = mm_nt(values, target).astype(jnp.int32)


def by_tile(owners, value_ref, high_ref, low_ref, start):
    size = value_ref.shape[0]
    per = size // owners
    strip = per // TILES
    for t in range(TILES):
        for p in range(owners):
            high, low = halves(value_ref[p * per + t * strip : p * per + (t + 1) * strip, :])
            to = start + (t * owners + p) * strip
            high_ref[to : to + strip, :] = high
            low_ref[to : to + strip, :] = low


def local_body(owners, chunks, *refs):
    parts = refs[:chunks]
    ids_ref, high_ref, low_ref, lid_ref = refs[chunks:]
    size = parts[0].shape[0]
    for k in range(chunks):
        by_tile(owners, parts[k], high_ref, low_ref, k * size)
    for b in range(chunks * size // LANES):
        row = ids_ref[:, b * LANES : (b + 1) * LANES].astype(jnp.float32)
        wide = jnp.transpose(jnp.broadcast_to(row, (LANES, LANES)))
        lid_ref[b * LANES : (b + 1) * LANES, :] = wide.astype(jnp.int32)


def gram_body(owners, items, last, level_ref, flag_ref, *refs):
    count = len(items)
    visitors = refs[:count]
    high_ref, low_ref, lid_ref, ids_ref, acc_ref, part_ref, acc_out, part_out = refs[count : count + 8]
    v_ref, vh_ref, vl_ref, col_ref, sem = refs[count + 8 :]
    size, _ = visitors[0].shape
    slots = high_ref.shape[0]
    tile = size // TILES
    blocks = slots // tile
    acc_out[...] = acc_ref[...]
    part_out[...] = part_ref[...]

    def fetch(n):
        return pltpu.make_async_copy(visitors[n], v_ref.at[n], sem.at[n])

    for n, (at, k) in enumerate(items):

        @pl.when(level_ref[at] >= 0)
        def _(n=n):
            fetch(n).start()

    for n, (at, k) in enumerate(items):

        @pl.when(level_ref[at] >= 0)
        def _(n=n, at=at, k=k):
            fetch(n).wait()
            by_tile(owners, v_ref.at[n], vh_ref, vl_ref, 0)
            col_ref[...] = jnp.zeros_like(col_ref)
            level = level_ref[at]
            first = level * (slots // tile) + k * TILES

            def step(i, _):
                t = i // blocks
                b = i - t * blocks

                @pl.when(flag_ref[(first + t) * blocks + b] > 0)
                def _():
                    rows = pl.ds(pl.multiple_of(b * tile, tile), tile)
                    cols = pl.ds(pl.multiple_of(t * tile, tile), tile)
                    left_h = high_ref[rows, :]
                    right_h = vh_ref[cols, :]
                    score = mm_nt(left_h, right_h) + mm_nt(left_h, vl_ref[cols, :]) + mm_nt(low_ref[rows, :], right_h)
                    lid = lid_ref[rows, :]
                    vid = ids_ref[first + t]
                    row_part = acc_out[rows, :]
                    for c in range(tile // LANES):
                        lanes = slice(c * LANES, (c + 1) * LANES)
                        weight = jnp.exp(SHARPNESS * (score[:, lanes] - 1.0))
                        weight = jnp.where(lid == vid[:, lanes], weight, 0.0)
                        row_part = row_part + weight
                        col_ref[t, :, lanes] += jnp.sum(weight.reshape(tile // 8, 8, LANES), axis=0)
                    acc_out[rows, :] = row_part

                return 0

            lax.fori_loop(0, TILES * blocks, step, 0)
            if at > 0:
                for t in range(TILES):
                    where = slice(k * size + t * tile, k * size + (t + 1) * tile)
                    part_out[pl.ds(level, 1), where] += jnp.sum(col_ref[t], axis=0, keepdims=True)

    if last:
        first, rest = halves(acc_out[...])
        second, _ = halves(acc_out[...] - first.astype(jnp.float32) - rest.astype(jnp.float32))
        ones = jnp.ones((8, LANES), jnp.bfloat16)
        total = mm_nt(ones, first) + mm_nt(ones, rest) + mm_nt(ones, second)
        part_out[pl.ds(level_ref[0], 1), :] += total[0:1, :]


def last_body(levels, owners, mass_ref, q_ref, score_ref):
    mass = mass_ref[0:owners, :]
    for z in range(1, levels):
        mass = mass + mass_ref[z * owners : (z + 1) * owners, :]
    cap = mass.shape[1]
    owner = q_ref[0:1, :]
    rank = q_ref[1:2, :]
    rows = owner.shape[1]
    at_rank = hot(iota((cap, rows), 0) == rank)
    first = mass.astype(jnp.bfloat16)
    rest = mass - first.astype(jnp.float32)
    second, third = halves(rest)
    value = mm(first, at_rank) + mm(second, at_rank) + mm(third, at_rank)
    mine = iota((owners, rows), 0) == owner
    score_ref[...] = jnp.log(jnp.sum(jnp.where(mine, value, 0.0), axis=0, keepdims=True))


def body(embeddings, cluster_ids, owner_map, source_order):
    rows, width = embeddings.shape
    clusters = owner_map.shape[0]
    levels = lax.axis_size("outer")
    inner = lax.axis_size("inner")
    groups = lax.axis_size("grp")
    owners = levels * inner
    held = clusters // owners
    cap = 2 * rows // owners
    per = cap // CHUNKS
    size = owners * per
    slots = CHUNKS * size
    ids = cluster_ids.reshape(1, rows)
    om = owner_map.reshape(clusters, 1)
    omr = owner_map.reshape(1, clusters)
    bf, i32 = jnp.bfloat16, jnp.int32

    first, high, low, info, sid = call(
        functools.partial(front_body, owners, per),
        (out((size, width)), out((rows, width), bf), out((rows, width), bf), out((8, rows), i32), out((owners, cap), i32)),
        embeddings, ids, om, omr, micros=5,
    )
    back = call(
        functools.partial(back_body, owners, per, CHUNKS, held),
        tuple(out((size, width)) for _ in range(CHUNKS - 1)) + (out((clusters, width)), out((8, rows), i32)),
        high, low, info, ids, om, omr, source_order.reshape(1, rows), micros=6,
    )
    sends = (first,) + tuple(back[: CHUNKS - 1])
    sums, q_info = back[CHUNKS - 1 :]

    tile = size // TILES
    strip = per // TILES
    blocks = slots // tile

    def to_owner(value):
        got = lax.all_to_all(value.reshape(owners, per, width), PLANE, 0, 0, tiled=True)
        return got.reshape(size, width)

    all_ids = lax.all_to_all(jnp.tile(sid, (levels, 1)), BY_LEVEL, 0, 0, tiled=True)
    mine = []
    for k in range(CHUNKS):
        send = sends[k] if k == 0 else lax.optimization_barrier((sends[k], mine[-1]))[0]
        mine.append(to_owner(send))
    all_ids = all_ids.reshape(levels, owners, CHUNKS, TILES, strip).transpose(0, 2, 3, 1, 4)
    all_ids = all_ids.reshape(levels * blocks, 1, tile)

    level = lax.axis_index("outer")
    down = lax.axis_index("inner") % 2
    seat = jnp.where(down == 1, levels - 1 - level, level)

    def pairs(moves):
        found = []
        for lane in range(inner):
            for a, b in moves:
                if lane % 2:
                    a, b = levels - 1 - a, levels - 1 - b
                found.append((a * inner + lane, b * inner + lane))
        return found

    top = levels - 1
    moves = []
    for s in range(1, top + 1):
        moves.append([(a, a + 1) for a in range(s - 1, top) if not (s == 1 and a == top - 1)])
    back_move = [(top, top - 1)]

    arrived = {}
    for k in range(CHUNKS):
        value = mine[k]
        for s in range(1, top + 1):
            value = lax.ppermute(value, LINE, pairs(moves[s - 1]))
            arrived[s, k] = value
        arrived["b", k] = lax.ppermute(mine[k], LINE, pairs(back_move))

    keys = [1, "b"] + list(range(2, top + 1))

    def source_seat(key):
        if key == "b":
            return jnp.where(seat == top - 1, top, -1)
        got = seat >= key
        if key == 1:
            got = got & (seat < top)
        return jnp.where(got, seat - key, -1)

    seats = [seat] + [source_seat(key) for key in keys]
    level_of = jnp.stack([jnp.where(a < 0, -1, jnp.where(down == 1, top - a, a)) for a in seats]).astype(i32)
    low_id = jnp.min(jnp.where(all_ids < 0, clusters, all_ids), axis=(1, 2))
    high_id = jnp.max(all_ids, axis=(1, 2))
    own_ids = lax.dynamic_slice_in_dim(all_ids, level * blocks, blocks, 0)
    own_low = lax.dynamic_slice_in_dim(low_id, level * blocks, blocks, 0)
    own_high = lax.dynamic_slice_in_dim(high_id, level * blocks, blocks, 0)
    flags = (low_id[:, None] <= own_high[None, :]) & (own_low[None, :] <= high_id[:, None])
    flags = flags.astype(i32).reshape(-1)
    lh, ll, lid = call(
        functools.partial(local_body, owners, CHUNKS),
        (out((slots, width), bf), out((slots, width), bf), out((slots, LANES), i32)),
        *mine, own_ids.reshape(1, slots), micros=5,
    )

    def finish(sums):
        piece = lax.all_to_all(sums.reshape(owners, held, width), PLANE, 0, 0, tiled=True)
        piece = jnp.sum(piece, axis=0)
        total = None
        for s in range(groups):
            route = [(g * levels + z, ((z + s) % groups) * levels + g) for g in range(groups) for z in range(levels)]
            got = lax.ppermute(piece, ("grp", "outer"), route)
            total = got if total is None else total + got
        return total * lax.rsqrt(jnp.mean(total * total, axis=1, keepdims=True) + 1e-6)

    centroids = finish(lax.optimization_barrier((sums, mine[0]))[0])
    acc = jnp.zeros((slots, LANES), jnp.float32)
    part = jnp.zeros((levels, slots), jnp.float32)

    def gram(acc, part, items, after, last, micros):
        flag = flags
        for value in after:
            flag = lax.optimization_barrier((flag, value))[0]
        visitors = [mine[k] if key == "own" else arrived[key, k] for key, k in items]
        at = tuple((0 if key == "own" else 1 + keys.index(key), k) for key, k in items)
        count = len(items)
        vm = pl.BlockSpec(memory_space=VMEM)
        return pl.pallas_call(
            functools.partial(gram_body, owners, at, last),
            out_shape=(out((slots, LANES)), out((levels, slots))),
            in_specs=[pl.BlockSpec(memory_space=pltpu.SMEM)] * 2 + [pl.BlockSpec(memory_space=pl.ANY)] * count + [vm] * 6,
            out_specs=(vm, vm),
            scratch_shapes=[
                VMEM((count, size, width), jnp.float32),
                VMEM((size, width), bf),
                VMEM((size, width), bf),
                VMEM((TILES, 8, tile), jnp.float32),
                pltpu.SemaphoreType.DMA((count,)),
            ],
            cost_estimate=cost(micros),
            name="gram",
        )(level_of, flag, *visitors, lh, ll, lid, all_ids, acc, part)

    plan = [
        ([("own", k) for k in range(CHUNKS)], [(1, 1), (2, 0)], 10),
        ([(1, 0), ("b", 0), (2, 0), (1, 1)], [(1, 2), (2, 1)], 12),
        ([("b", 1), (2, 1), (1, 2), ("b", 2), (3, 0)], [(2, 2)], 12),
        ([(2, 2), (3, 1)], [], 7),
        ([(3, 2)], [], 5),
    ]
    for n, (items, after, micros) in enumerate(plan):
        last = n == len(plan) - 1
        acc, part = gram(acc, part, items, [], last, micros)
    parts = part.reshape(levels, CHUNKS, TILES, owners, strip).transpose(0, 3, 1, 2, 4).reshape(levels * owners, cap)
    home = lax.all_to_all(parts, BY_LEVEL, 0, 0, tiled=True)
    score = call(functools.partial(last_body, levels, owners), out((1, rows)), home, q_info, micros=2)

    return score.reshape(rows), centroids


def solution(mesh):
    groups, owned = mesh.shape["grp"], mesh.shape["own"]
    split = Mesh(mesh.devices.reshape(groups, groups, owned // groups), EVERY)
    return jax.shard_map(
        body,
        mesh=split,
        in_specs=(P(EVERY, None), P(EVERY), P(), P(EVERY)),
        out_specs=(P(EVERY), P(LINE, None)),
        check_vma=False,
    )
```

```python
import functools
import math

import jax
import jax.numpy as jnp
from jax import lax
from jax.experimental import pallas as pl
from jax.experimental.pallas import tpu as pltpu
from jax.sharding import Mesh
from jax.sharding import PartitionSpec as P


SHARPNESS = 6.0
SCALE = (SHARPNESS * 1.4426950408889634) ** 0.5
CHUNKS = 3
TILES = 2
LANES = 128
VMEM = pltpu.VMEM
EVERY = ("grp", "outer", "inner")
PLANE = ("grp", "inner")
LINE = ("outer", "inner")
BY_LEVEL = ("outer", "grp", "inner")
NT = (((1,), (1,)), ((), ()))


def iota(shape, axis):
    return lax.broadcasted_iota(jnp.int32, shape, axis)


def mm(left, right):
    return jnp.dot(left, right, preferred_element_type=jnp.float32)


def mm_nt(left, right):
    return lax.dot_general(left, right, NT, preferred_element_type=jnp.float32)


def halves(value):
    high = value.astype(jnp.bfloat16)
    low = (value - high.astype(jnp.float32)).astype(jnp.bfloat16)
    return high, low


def hot(mask):
    return jnp.where(mask, 1.0, 0.0).astype(jnp.bfloat16)


def cost(micros):
    return pl.CostEstimate(flops=int(micros * 1.1e9), transcendentals=0, bytes_accessed=0)


def call(body, outs, *args, micros, scratch=(), smem=0, aliases=None):
    spec = [pl.BlockSpec(memory_space=pltpu.SMEM)] * smem
    spec += [pl.BlockSpec(memory_space=VMEM)] * (len(args) - smem)
    return pl.pallas_call(
        body,
        out_shape=outs,
        in_specs=spec,
        out_specs=jax.tree.map(lambda _: pl.BlockSpec(memory_space=VMEM), outs),
        scratch_shapes=list(scratch),
        input_output_aliases=aliases or {},
        cost_estimate=cost(micros),
    )(*args)


def out(shape, dtype=jnp.float32):
    return jax.ShapeDtypeStruct(shape, dtype)


def chunk_rows(owner, rank, high, low, k, owners, per):
    inside = (rank >= k * per) & (rank < (k + 1) * per)
    dest = jnp.where(inside, owner * per + rank - k * per, -1)
    pick = hot(iota((owners * per, dest.shape[1]), 0) == dest)
    return mm(pick, high) + mm(pick, low)


def front_body(owners, per, cap, x_ref, ids_ref, om_ref, chunk_ref, high_ref, low_ref, info_ref):
    x = x_ref[...]
    rows, width = x.shape
    clusters = om_ref.shape[0]
    ids = ids_ref[...].reshape(1, rows)
    square = (clusters, clusters)
    om_row = jnp.broadcast_to(om_ref[...].reshape(1, clusters), square)
    om_col = jnp.transpose(om_row.astype(jnp.float32)).astype(jnp.int32)
    om = om_col[:, 0:1]
    here = iota((clusters, rows), 0) == ids
    owner = jnp.sum(jnp.where(here, om, 0), axis=0, keepdims=True)
    mine = iota((owners, rows), 0) == owner
    member = hot(here)
    within = mm(member, hot(iota((rows, rows), 0) < iota((rows, rows), 1)))
    earlier = (om_col == om_row) & (iota(square, 1) < iota(square, 0))
    base = jnp.sum(mm(hot(earlier), member), axis=1, keepdims=True)
    rank = jnp.sum(jnp.where(here, within + base, 0.0), axis=0, keepdims=True)
    count = jnp.sum(mine.astype(jnp.float32), axis=1, keepdims=True)
    count = jnp.sum(jnp.where(mine, count, 0.0), axis=0, keepdims=True)
    rank = jnp.floor((rank * cap + 0.5) / count).astype(jnp.int32)
    order = om * (clusters // owners) + jnp.sum(earlier.astype(jnp.int32), axis=1, keepdims=True)
    position = jnp.sum(jnp.where(here, order, 0), axis=0, keepdims=True)
    info_ref[...] = jnp.concatenate([owner, rank, position, position] * 2, axis=0)
    unit = x * lax.rsqrt(jnp.sum(x * x, axis=1, keepdims=True) + 1e-6)
    high, low = halves(unit)
    high_ref[...] = high
    low_ref[...] = low
    chunk_ref[:, 0:per, :] = chunk_rows(owner, rank, high, low, 0, owners, per).reshape(owners, per, width)
    at_rank = hot(iota((width, rows), 0) == rank)
    coarse = (ids + 1) // 16
    fine = ids + 1 - coarse * 16
    coarse = jnp.where(mine, coarse.astype(jnp.float32), 0.0).astype(jnp.bfloat16)
    fine = jnp.where(mine, fine.astype(jnp.float32), 0.0).astype(jnp.bfloat16)
    sid = mm_nt(coarse, at_rank) * 16.0 + mm_nt(fine, at_rank) - 1.0
    for p in range(owners):
        chunk_ref[p, per:, :] = jnp.broadcast_to(sid[p : p + 1, :], chunk_ref[p, per:, :].shape)


def back_body(owners, per, chunks, held, high_ref, low_ref, info_ref, so_ref, *outs):
    high = high_ref[...]
    low = low_ref[...]
    owner = info_ref[0:1, :]
    rank = info_ref[1:2, :]
    position = info_ref[2:3, :]
    rows, width = high.shape
    clusters = owners * held
    pick = hot(iota((clusters, rows), 0) == position)
    sums = (mm(pick, high) + mm(pick, low)).reshape(owners, held, width)
    share = held // (chunks - 1)
    for k in range(1, chunks):
        outs[k - 1][:, 0:per, :] = chunk_rows(owner, rank, high, low, k, owners, per).reshape(owners, per, width)
        outs[k - 1][:, per:, :] = sums[:, (k - 1) * share : k * share, :]
    q_ref = outs[chunks - 1]
    target = hot(iota((rows, rows), 0) == so_ref[...].reshape(1, rows))
    values = info_ref[...].astype(jnp.float32).astype(jnp.bfloat16)
    q_ref[...] = mm_nt(values, target).astype(jnp.int32)


def by_tile(owners, value_ref, high_ref, low_ref, start):
    size = value_ref.shape[0]
    per = size // owners
    strip = per // TILES
    for t in range(TILES):
        for p in range(owners):
            rows = value_ref[p * per + t * strip : p * per + (t + 1) * strip, :]
            high, low = halves(rows * SCALE)
            to = start + (t * owners + p) * strip
            high_ref[to : to + strip, :] = high
            low_ref[to : to + strip, :] = low


def tick_body(value_ref, tick_ref):
    tick_ref[...] = jnp.zeros_like(tick_ref)


def meta_body(owners, chunks, *refs):
    count = len(refs) - 3
    ids_out, flag_out = refs[count + 1 :]
    cap = refs[0].shape[1]
    blocks = chunks * TILES
    tile = ids_out.shape[3]
    strip = cap // blocks
    slots = blocks * tile
    ids = jnp.concatenate([ref[...] for ref in refs[:count]], axis=0)
    coarse = jnp.floor(ids * 0.0625)
    fine = ids - coarse * 16.0
    lane = iota((cap, slots), 1)
    spread = hot(iota((cap, slots), 0) == lane // tile * strip + lane % strip)
    wide = mm(coarse.astype(jnp.bfloat16), spread) * 16.0 + mm(fine.astype(jnp.bfloat16), spread)
    sender = iota((owners, slots), 1) % tile // strip == iota((owners, slots), 0)
    flag_lane = iota((1, LANES), 1)
    ends = []
    for key in range(count):
        row = jnp.sum(jnp.where(sender, wide[key * owners : (key + 1) * owners, :], 0.0), axis=0, keepdims=True)
        found = []
        for t in range(blocks):
            part = row[:, t * tile : (t + 1) * tile]
            ids_out[key, t] = part
            least = jnp.min(jnp.where(part < 0.0, 1e6, part), axis=1, keepdims=True)
            found.append((least, jnp.max(part, axis=1, keepdims=True)))
        ends.append(found)
        flags = jnp.zeros((1, LANES), jnp.int32)
        for t in range(blocks):
            for b in range(blocks):
                met = (found[t][0] <= ends[0][b][1]) & (ends[0][b][0] <= found[t][1])
                flags = jnp.where((flag_lane == t * blocks + b) & met, 1, flags)
        flag_out[key : key + 1, :] = flags
    flag_out[count:, :] = jnp.zeros((flag_out.shape[0] - count, LANES), jnp.int32)


def gram_body(owners, items, own, level_ref, flag_ref, *refs):
    count = len(items)
    visitors = refs[:count]
    refs = refs[count:]
    if own:
        ids_ref, part_ref, part_out, high_ref, low_ref, lid_ref = refs[:6]
        acc_ref, v_ref, col_ref, pair_ref, sem = refs[6:]
        vh_ref, vl_ref = high_ref, low_ref
    else:
        high_any, low_any, lid_any, ids_ref, part_ref, part_out = refs[:6]
        acc_ref, v_ref, col_ref, pair_ref, sem, high_ref, low_ref, lid_ref, vh_ref, vl_ref, own_sem = refs[6:]
    size = v_ref.shape[1]
    slots = high_ref.shape[0]
    tile = size // TILES
    blocks = slots // tile
    part_out[...] = part_ref[...]
    alive = level_ref[items[0][0]] >= 0
    for at, k in items[1:]:
        alive = alive | (level_ref[at] >= 0)

    def fetch(n):
        return pltpu.make_async_copy(visitors[n], v_ref.at[n], sem.at[n])

    for n, (at, k) in enumerate(items):

        @pl.when(level_ref[at] >= 0)
        def _(n=n):
            fetch(n).start()

    held = []
    if not own:
        for n, (source, target) in enumerate(((high_any, high_ref), (low_any, low_ref), (lid_any, lid_ref))):
            held.append(pltpu.make_async_copy(source, target, own_sem.at[n]))

    @pl.when(alive)
    def _():
        for copy in held:
            copy.start()
        acc_ref[...] = jnp.zeros_like(acc_ref)
        col_ref[...] = jnp.zeros_like(col_ref)
        if own:
            for b in range(slots // LANES):
                row = ids_ref[0, b * LANES // tile, :, b * LANES % tile : b * LANES % tile + LANES]
                lid_ref[b * LANES : (b + 1) * LANES, :] = jnp.transpose(jnp.broadcast_to(row, (LANES, LANES)))

    total = jnp.int32(0)
    for n, (at, k) in enumerate(items):
        live = level_ref[at] >= 0
        for t in range(TILES):
            begin, end = jnp.int32(blocks), jnp.int32(-1)
            for b in range(blocks):
                met = flag_ref[at, (k * TILES + t) * blocks + b] > 0
                if own and b < k * TILES + t:
                    continue
                begin = jnp.where(met, jnp.minimum(begin, b), begin)
                end = jnp.where(met, b, end)
            for w in range((blocks + 1) // 2):
                start = begin + 2 * w
                used = jnp.minimum(start, blocks - 2)
                pair_ref[0, total] = used
                pair_ref[1, total] = n * TILES + t
                pair_ref[2, total] = k * TILES + t
                pair_ref[3, total] = at
                pair_ref[4, total] = (used == start).astype(jnp.int32)
                pair_ref[5, total] = (used < end).astype(jnp.int32)
                total = total + (live & (start <= end)).astype(jnp.int32)

    for n, (at, k) in enumerate(items):

        @pl.when(level_ref[at] >= 0)
        def _(n=n):
            fetch(n).wait()
            by_tile(owners, v_ref.at[n], vh_ref, vl_ref, n * size)

    @pl.when(alive)
    def _():
        for copy in held:
            copy.wait()

        def step(i, _):
            b = pair_ref[0, i]
            v = pair_ref[1, i]
            vid = ids_ref[pair_ref[3, i], pair_ref[2, i]]
            rows = pl.ds(pl.multiple_of(b * tile, tile), 2 * tile)
            cols = pl.ds(pl.multiple_of(v * tile, tile), tile)
            left_h = high_ref[rows, :]
            right_h = vh_ref[cols, :]
            left = jnp.concatenate([left_h, left_h, low_ref[rows, :]], axis=1)
            right = jnp.concatenate([right_h, vl_ref[cols, :], right_h], axis=1)
            score = mm_nt(left, right)
            for h in range(2):
                half = pl.ds(pl.multiple_of((b + h) * tile, tile), tile)
                lid = lid_ref[half, :]
                row_part = acc_ref[half, :]
                wanted = vid + jnp.where(pair_ref[4 + h, i] > 0, 0.0, 1e6)
                for c in range(tile // LANES):
                    lanes = slice(c * LANES, (c + 1) * LANES)
                    weight = jnp.exp2(score[h * tile : (h + 1) * tile, lanes])
                    weight = jnp.where(lid == wanted[:, lanes], weight, 0.0)
                    row_part = row_part + weight
                    col = jnp.sum(weight.reshape(tile // 8, 8, LANES), axis=0)
                    col_ref[v, :, lanes] += col * jnp.where(b + h > v, 1.0, 0.0) if own else col
                acc_ref[half, :] = row_part
            return 0

        lax.fori_loop(0, total, step, 0)
        first, rest = halves(acc_ref[...])
        second, _ = halves(acc_ref[...] - first.astype(jnp.float32) - rest.astype(jnp.float32))
        ones = jnp.ones((8, LANES), jnp.bfloat16)
        rows = mm_nt(ones, first) + mm_nt(ones, rest) + mm_nt(ones, second)
        part_out[pl.ds(level_ref[0], 1), :] += rows[0:1, :]

    for n, (at, k) in enumerate(items):

        @pl.when(level_ref[at] >= 0)
        def _(n=n, at=at, k=k):
            for t in range(TILES):
                where = slice(k * size + t * tile, k * size + (t + 1) * tile)
                part_out[pl.ds(level_ref[at], 1), where] += jnp.sum(col_ref[n * TILES + t], axis=0, keepdims=True)


def last_body(levels, owners, mass_ref, q_ref, score_ref):
    mass = mass_ref[0:owners, :]
    for z in range(1, levels):
        mass = mass + mass_ref[z * owners : (z + 1) * owners, :]
    cap = mass.shape[1]
    owner = q_ref[0:1, :]
    rank = q_ref[1:2, :]
    rows = owner.shape[1]
    at_rank = hot(iota((cap, rows), 0) == rank)
    first = mass.astype(jnp.bfloat16)
    rest = mass - first.astype(jnp.float32)
    second, third = halves(rest)
    value = mm(first, at_rank) + mm(second, at_rank) + mm(third, at_rank)
    mine = iota((owners, rows), 0) == owner
    total = jnp.sum(jnp.where(mine, value, 0.0), axis=0, keepdims=True)
    score_ref[...] = jnp.log(total * math.exp(-SHARPNESS))


def body(embeddings, cluster_ids, owner_map, source_order):
    rows, width = embeddings.shape
    clusters = owner_map.shape[0]
    levels = lax.axis_size("outer")
    inner = lax.axis_size("inner")
    groups = lax.axis_size("grp")
    owners = levels * inner
    held = clusters // owners
    cap = 2 * rows // owners
    per = cap // CHUNKS
    size = owners * per
    slots = CHUNKS * size
    share = held // (CHUNKS - 1)
    bf, i32 = jnp.bfloat16, jnp.int32
    dealt = out((owners, per + share, width))

    first, high, low, info = call(
        functools.partial(front_body, owners, per, cap),
        (dealt, out((rows, width), bf), out((rows, width), bf), out((8, rows), i32)),
        embeddings, cluster_ids, owner_map, micros=5,
    )
    back = call(
        functools.partial(back_body, owners, per, CHUNKS, held),
        (dealt,) * (CHUNKS - 1) + (out((8, rows), i32),),
        high, low, info, source_order, micros=6,
    )
    sends = (first,) + tuple(back[: CHUNKS - 1])
    q_info = back[CHUNKS - 1]
    tile = size // TILES
    strip = per // TILES
    blocks = slots // tile

    got, mine = [], []
    for k in range(CHUNKS):
        send = sends[k] if k == 0 else lax.optimization_barrier((sends[k], mine[-1]))[0]
        got.append(lax.all_to_all(send, PLANE, 0, 0, tiled=True))
        mine.append(got[k][:, :per, :].reshape(size, width))
    own_ids = got[0][:, per, :cap].reshape(owners, cap)
    piece = jnp.concatenate([jnp.sum(got[k][:, per:, :], axis=0) for k in range(1, CHUNKS)], axis=0)

    level = lax.axis_index("outer")
    down = lax.axis_index("inner") % 2
    seat = jnp.where(down == 1, levels - 1 - level, level)

    def pairs(moves):
        found = []
        for lane in range(inner):
            for a, b in moves:
                if lane % 2:
                    a, b = levels - 1 - a, levels - 1 - b
                found.append((a * inner + lane, b * inner + lane))
        return found

    top = levels - 1
    moves = []
    for s in range(1, top + 1):
        moves.append([(a, a + 1) for a in range(s - 1, top) if not (s == 1 and a == top - 1)])
    back_move = [(top, top - 1)]

    arrived = {}

    def direct(steps):
        return [(a, a + steps) for a in range(top + 1 - steps) if not (steps == 1 and a == top - 1)]

    ids_of = [own_ids]
    for s in range(1, top + 1):
        ids_of.append(lax.ppermute(own_ids, LINE, pairs(direct(s))))
    ids_of.insert(2, lax.ppermute(own_ids, LINE, pairs(back_move)))
    for k in range(CHUNKS):
        value = mine[k]
        for s in range(1, top + 1):
            value = lax.ppermute(value, LINE, pairs(moves[s - 1]))
            arrived[s, k] = value
        arrived["b", k] = lax.ppermute(mine[k], LINE, pairs(back_move))

    tick = pl.pallas_call(
        tick_body,
        out_shape=out((8, LANES)),
        in_specs=[pl.BlockSpec(memory_space=pl.ANY)],
        out_specs=pl.BlockSpec(memory_space=VMEM),
        name="tick",
    )(arrived[1, 0])
    keys_held = len(ids_of)
    ids, flags = call(
        functools.partial(meta_body, owners, CHUNKS),
        (out((keys_held, blocks, 1, tile)), out((8, LANES), i32)),
        *ids_of, tick, micros=3,
    )
    keys = [1, "b"] + list(range(2, top + 1))

    def source_seat(key):
        if key == "b":
            return jnp.where(seat == top - 1, top, -1)
        got = seat >= key
        if key == 1:
            got = got & (seat < top)
        return jnp.where(got, seat - key, -1)

    seats = [seat] + [source_seat(key) for key in keys]
    level_of = jnp.stack([jnp.where(a < 0, -1, jnp.where(down == 1, top - a, a)) for a in seats]).astype(i32)
    part = jnp.zeros((levels, slots), jnp.float32)

    def gram(part, items, held, micros):
        own = not held
        visitors = [mine[k] if key == "own" else arrived[key, k] for key, k in items]
        at = tuple((0 if key == "own" else 1 + keys.index(key), k) for key, k in items)
        count = len(items)
        vm = pl.BlockSpec(memory_space=VMEM)
        any_ = pl.BlockSpec(memory_space=pl.ANY)
        own_out = (out((slots, width), bf), out((slots, width), bf), out((slots, LANES)))
        scratch = [
            VMEM((slots, LANES), jnp.float32),
            VMEM((count, size, width), jnp.float32),
            VMEM((count * TILES, 8, tile), jnp.float32),
            pltpu.SMEM((6, count * TILES * blocks + 1), i32),
            pltpu.SemaphoreType.DMA((count,)),
        ]
        if not own:
            scratch += [
                VMEM((slots, width), bf),
                VMEM((slots, width), bf),
                VMEM((slots, LANES), jnp.float32),
                VMEM((count * size, width), bf),
                VMEM((count * size, width), bf),
                pltpu.SemaphoreType.DMA((3,)),
            ]
        return pl.pallas_call(
            functools.partial(gram_body, owners, at, own),
            out_shape=(out((levels, slots)),) + (own_out if own else ()),
            in_specs=[pl.BlockSpec(memory_space=pltpu.SMEM)] * 2 + [any_] * (count + len(held)) + [vm] * 2,
            out_specs=(vm,) * (4 if own else 1),
            scratch_shapes=scratch,
            cost_estimate=cost(micros),
            name="gram",
        )(level_of, flags, *visitors, *held, ids, part)

    plan = [
        ([("own", k) for k in range(CHUNKS)], 10),
        ([(1, 0), ("b", 0), (2, 0), (1, 1)], 12),
        ([("b", 1), (2, 1), (1, 2)], 10),
        ([("b", 2), (2, 2), (3, 0)], 9),
        ([(3, 1)], 5),
        ([(3, 2)], 5),
    ]
    held_here = ()
    for n, (items, micros) in enumerate(plan):
        part, *made = gram(part, items, held_here, micros)
        held_here = held_here or tuple(made)
        if n == 2:
            piece = lax.optimization_barrier((piece, part))[0]
    total = None
    for s in range(groups):
        route = [(g * levels + z, ((z + s) % groups) * levels + g) for g in range(groups) for z in range(levels)]
        came = lax.ppermute(piece, ("grp", "outer"), route)
        total = came if total is None else total + came
    centroids = total * lax.rsqrt(jnp.mean(total * total, axis=1, keepdims=True) + 1e-6)
    parts = part.reshape(levels, CHUNKS, TILES, owners, strip).transpose(0, 3, 1, 2, 4).reshape(levels * owners, cap)
    home = lax.all_to_all(parts, BY_LEVEL, 0, 0, tiled=True)
    score = call(functools.partial(last_body, levels, owners), out((1, rows)), home, q_info, micros=2)

    return score.reshape(rows), centroids


def solution(mesh):
    groups, owned = mesh.shape["grp"], mesh.shape["own"]
    split = Mesh(mesh.devices.reshape(groups, groups, owned // groups), EVERY)
    return jax.shard_map(
        body,
        mesh=split,
        in_specs=(P(EVERY, None), P(EVERY), P(), P(EVERY)),
        out_specs=(P(EVERY), P(LINE, None)),
        check_vma=False,
    )
```

```python
import functools
import math

import jax
import jax.numpy as jnp
from jax import lax
from jax.experimental import pallas as pl
from jax.experimental.pallas import tpu as pltpu
from jax.sharding import Mesh
from jax.sharding import PartitionSpec as P


SHARPNESS = 6.0
SCALE = (SHARPNESS * 1.4426950408889634) ** 0.5
CHUNKS = 3
TILES = 2
LANES = 128
VMEM = pltpu.VMEM
EVERY = ("grp", "outer", "inner")
PLANE = ("grp", "inner")
LINE = ("outer", "inner")
BY_LEVEL = ("outer", "grp", "inner")
NT = (((1,), (1,)), ((), ()))


def iota(shape, axis):
    return lax.broadcasted_iota(jnp.int32, shape, axis)


def mm(left, right):
    return jnp.dot(left, right, preferred_element_type=jnp.float32)


def mm_nt(left, right):
    return lax.dot_general(left, right, NT, preferred_element_type=jnp.float32)


def halves(value):
    high = value.astype(jnp.bfloat16)
    low = (value - high.astype(jnp.float32)).astype(jnp.bfloat16)
    return high, low


def hot(mask):
    return jnp.where(mask, 1.0, 0.0).astype(jnp.bfloat16)


def cost(micros):
    return pl.CostEstimate(flops=int(micros * 1.1e9), transcendentals=0, bytes_accessed=0)


def call(body, outs, *args, micros, scratch=(), smem=0, aliases=None):
    spec = [pl.BlockSpec(memory_space=pltpu.SMEM)] * smem
    spec += [pl.BlockSpec(memory_space=VMEM)] * (len(args) - smem)
    return pl.pallas_call(
        body,
        out_shape=outs,
        in_specs=spec,
        out_specs=jax.tree.map(lambda _: pl.BlockSpec(memory_space=VMEM), outs),
        scratch_shapes=list(scratch),
        input_output_aliases=aliases or {},
        cost_estimate=cost(micros),
    )(*args)


def out(shape, dtype=jnp.float32):
    return jax.ShapeDtypeStruct(shape, dtype)


def chunk_rows(owner, rank, high, low, k, owners, per):
    inside = (rank >= k * per) & (rank < (k + 1) * per)
    dest = jnp.where(inside, owner * per + rank - k * per, -1)
    pick = hot(iota((owners * per, dest.shape[1]), 0) == dest)
    return mm(pick, high) + mm(pick, low)


def front_body(owners, per, cap, x_ref, ids_ref, om_ref, chunk_ref, high_ref, low_ref, info_ref):
    x = x_ref[...]
    rows, width = x.shape
    clusters = om_ref.shape[0]
    ids = ids_ref[...].reshape(1, rows)
    square = (clusters, clusters)
    om_row = jnp.broadcast_to(om_ref[...].reshape(1, clusters), square)
    om_col = jnp.transpose(om_row.astype(jnp.float32)).astype(jnp.int32)
    om = om_col[:, 0:1]
    here = iota((clusters, rows), 0) == ids
    owner = jnp.sum(jnp.where(here, om, 0), axis=0, keepdims=True)
    mine = iota((owners, rows), 0) == owner
    member = hot(here)
    within = mm(member, hot(iota((rows, rows), 0) < iota((rows, rows), 1)))
    earlier = (om_col == om_row) & (iota(square, 1) < iota(square, 0))
    base = jnp.sum(mm(hot(earlier), member), axis=1, keepdims=True)
    rank = jnp.sum(jnp.where(here, within + base, 0.0), axis=0, keepdims=True)
    count = jnp.sum(mine.astype(jnp.float32), axis=1, keepdims=True)
    count = jnp.sum(jnp.where(mine, count, 0.0), axis=0, keepdims=True)
    rank = jnp.floor((rank * cap + 0.5) / count).astype(jnp.int32)
    order = om * (clusters // owners) + jnp.sum(earlier.astype(jnp.int32), axis=1, keepdims=True)
    position = jnp.sum(jnp.where(here, order, 0), axis=0, keepdims=True)
    info_ref[...] = jnp.concatenate([owner, rank, position, position] * 2, axis=0)
    unit = x * lax.rsqrt(jnp.sum(x * x, axis=1, keepdims=True) + 1e-6)
    high, low = halves(unit)
    high_ref[...] = high
    low_ref[...] = low
    chunk_ref[:, 0:per, :] = chunk_rows(owner, rank, high, low, 0, owners, per).reshape(owners, per, width)
    at_rank = hot(iota((width, rows), 0) == rank)
    coarse = (ids + 1) // 16
    fine = ids + 1 - coarse * 16
    coarse = jnp.where(mine, coarse.astype(jnp.float32), 0.0).astype(jnp.bfloat16)
    fine = jnp.where(mine, fine.astype(jnp.float32), 0.0).astype(jnp.bfloat16)
    sid = mm_nt(coarse, at_rank) * 16.0 + mm_nt(fine, at_rank) - 1.0
    for p in range(owners):
        chunk_ref[p, per:, :] = jnp.broadcast_to(sid[p : p + 1, :], chunk_ref[p, per:, :].shape)


def back_body(owners, per, chunks, held, high_ref, low_ref, info_ref, so_ref, *outs):
    high = high_ref[...]
    low = low_ref[...]
    owner = info_ref[0:1, :]
    rank = info_ref[1:2, :]
    position = info_ref[2:3, :]
    rows, width = high.shape
    clusters = owners * held
    pick = hot(iota((clusters, rows), 0) == position)
    sums = (mm(pick, high) + mm(pick, low)).reshape(owners, held, width)
    share = held // (chunks - 1)
    for k in range(1, chunks):
        outs[k - 1][:, 0:per, :] = chunk_rows(owner, rank, high, low, k, owners, per).reshape(owners, per, width)
        outs[k - 1][:, per:, :] = sums[:, (k - 1) * share : k * share, :]
    q_ref = outs[chunks - 1]
    target = hot(iota((rows, rows), 0) == so_ref[...].reshape(1, rows))
    values = info_ref[...].astype(jnp.float32).astype(jnp.bfloat16)
    q_ref[...] = mm_nt(values, target).astype(jnp.int32)


def by_tile(owners, value_ref, high_ref, low_ref, start):
    size = value_ref.shape[0]
    per = size // owners
    strip = per // TILES
    for t in range(TILES):
        for p in range(owners):
            rows = value_ref[p * per + t * strip : p * per + (t + 1) * strip, :]
            high, low = halves(rows * SCALE)
            to = start + (t * owners + p) * strip
            high_ref[to : to + strip, :] = high
            low_ref[to : to + strip, :] = low


def tick_body(value_ref, through_ref, out_ref):
    out_ref[...] = through_ref[...]


def meta_body(owners, chunks, *refs):
    count = len(refs) - 2
    ids_out, flag_out = refs[count:]
    cap = refs[0].shape[1]
    blocks = chunks * TILES
    tile = ids_out.shape[3]
    strip = cap // blocks
    slots = blocks * tile
    ids = jnp.concatenate([ref[...] for ref in refs[:count]], axis=0)
    coarse = jnp.floor(ids * 0.0625)
    fine = ids - coarse * 16.0
    lane = iota((cap, slots), 1)
    spread = hot(iota((cap, slots), 0) == lane // tile * strip + lane % strip)
    wide = mm(coarse.astype(jnp.bfloat16), spread) * 16.0 + mm(fine.astype(jnp.bfloat16), spread)
    sender = iota((owners, slots), 1) % tile // strip == iota((owners, slots), 0)
    flag_lane = iota((1, LANES), 1)
    ends = []
    for key in range(count):
        row = jnp.sum(jnp.where(sender, wide[key * owners : (key + 1) * owners, :], 0.0), axis=0, keepdims=True)
        found = []
        for t in range(blocks):
            part = row[:, t * tile : (t + 1) * tile]
            ids_out[key, t] = part
            least = jnp.min(jnp.where(part < 0.0, 1e6, part), axis=1, keepdims=True)
            found.append((least, jnp.max(part, axis=1, keepdims=True)))
        ends.append(found)
        flags = jnp.zeros((1, LANES), jnp.int32)
        for t in range(blocks):
            for b in range(blocks):
                met = (found[t][0] <= ends[0][b][1]) & (ends[0][b][0] <= found[t][1])
                flags = jnp.where((flag_lane == t * blocks + b) & met, 1, flags)
        flag_out[key : key + 1, :] = flags
    flag_out[count:, :] = jnp.zeros((flag_out.shape[0] - count, LANES), jnp.int32)


def gram_body(owners, items, own, held, level_ref, flag_ref, *refs):
    count = len(items)
    visitors = refs[:count]
    refs = refs[count:]
    kept = refs[:held]
    refs = refs[held:]
    if own:
        ids_ref, part_ref, part_out, high_out, low_out, lid_out = refs[:6] if held == 0 else refs[:5] + (None,)
        refs = refs[6 if held == 0 else 5 :]
    else:
        ids_ref, part_ref, part_out = refs[:3]
        refs = refs[3:]
    acc_ref, v_ref, col_ref, pair_ref, sem, high_ref, low_ref, lid_ref = refs[:8]
    if own:
        vh_ref, vl_ref = high_ref, low_ref
        own_sem = refs[8]
    else:
        vh_ref, vl_ref, own_sem = refs[8:]
    size = v_ref.shape[1]
    slots = high_ref.shape[0]
    tile = size // TILES
    blocks = slots // tile
    part_out[...] = part_ref[...]
    alive = level_ref[items[0][0]] >= 0
    for at, k in items[1:]:
        alive = alive | (level_ref[at] >= 0)

    def fetch(n):
        return pltpu.make_async_copy(visitors[n], v_ref.at[n], sem.at[n])

    for n, (at, k) in enumerate(items):

        @pl.when(level_ref[at] >= 0)
        def _(n=n):
            fetch(n).start()

    copies = []
    if held:
        early = kept[0].shape[0]
        places = [(kept[0], high_ref.at[0:early]), (kept[1], low_ref.at[0:early]), (kept[2], lid_ref)]
        if held > 3:
            places += [(kept[3], high_ref.at[early:slots]), (kept[4], low_ref.at[early:slots])]
        copies = [pltpu.make_async_copy(*place, own_sem.at[n]) for n, place in enumerate(places)]

    @pl.when(alive)
    def _():
        for copy in copies:
            copy.start()
        acc_ref[...] = jnp.zeros_like(acc_ref)
        col_ref[...] = jnp.zeros_like(col_ref)
        if own and held == 0:
            for b in range(slots // LANES):
                row = ids_ref[0, b * LANES // tile, :, b * LANES % tile : b * LANES % tile + LANES]
                lid_ref[b * LANES : (b + 1) * LANES, :] = jnp.transpose(jnp.broadcast_to(row, (LANES, LANES)))
            lid_out[...] = lid_ref[...]

    total = jnp.int32(0)
    for n, (at, k) in enumerate(items):
        live = level_ref[at] >= 0
        for t in range(TILES):
            begin, end = jnp.int32(blocks), jnp.int32(-1)
            for b in range(blocks):
                met = flag_ref[at, (k * TILES + t) * blocks + b] > 0
                if own and b > k * TILES + t:
                    continue
                begin = jnp.where(met, jnp.minimum(begin, b), begin)
                end = jnp.where(met, b, end)
            for w in range((blocks + 1) // 2):
                start = begin + 2 * w
                used = jnp.minimum(start, blocks - 2)
                pair_ref[0, total] = used
                pair_ref[1, total] = (k if own else n) * TILES + t
                pair_ref[2, total] = k * TILES + t
                pair_ref[3, total] = at
                pair_ref[4, total] = (used == start).astype(jnp.int32)
                pair_ref[5, total] = (used < end).astype(jnp.int32)
                total = total + (live & (start <= end)).astype(jnp.int32)

    for n, (at, k) in enumerate(items):

        @pl.when(level_ref[at] >= 0)
        def _(n=n):
            fetch(n).wait()
            by_tile(owners, v_ref.at[n], vh_ref, vl_ref, (items[n][1] if own else n) * size)

    @pl.when(alive)
    def _():
        for copy in copies:
            copy.wait()

        def step(i, _):
            b = pair_ref[0, i]
            v = pair_ref[1, i]
            vid = ids_ref[pair_ref[3, i], pair_ref[2, i]]
            rows = pl.ds(pl.multiple_of(b * tile, tile), 2 * tile)
            cols = pl.ds(pl.multiple_of(v * tile, tile), tile)
            left_h = high_ref[rows, :]
            right_h = vh_ref[cols, :]
            left = jnp.concatenate([left_h, left_h, low_ref[rows, :]], axis=1)
            right = jnp.concatenate([right_h, vl_ref[cols, :], right_h], axis=1)
            score = mm_nt(left, right)
            for h in range(2):
                half = pl.ds(pl.multiple_of((b + h) * tile, tile), tile)
                lid = lid_ref[half, :]
                row_part = acc_ref[half, :]
                wanted = vid + jnp.where(pair_ref[4 + h, i] > 0, 0.0, 1e6)
                for c in range(tile // LANES):
                    lanes = slice(c * LANES, (c + 1) * LANES)
                    weight = jnp.exp2(score[h * tile : (h + 1) * tile, lanes])
                    weight = jnp.where(lid == wanted[:, lanes], weight, 0.0)
                    row_part = row_part + weight
                    col = jnp.sum(weight.reshape(tile // 8, 8, LANES), axis=0)
                    col_ref[v, :, lanes] += col * jnp.where(b + h < v, 1.0, 0.0) if own else col
                acc_ref[half, :] = row_part
            return 0

        lax.fori_loop(0, total, step, 0)
        first, rest = halves(acc_ref[...])
        second, _ = halves(acc_ref[...] - first.astype(jnp.float32) - rest.astype(jnp.float32))
        ones = jnp.ones((8, LANES), jnp.bfloat16)
        rows = mm_nt(ones, first) + mm_nt(ones, rest) + mm_nt(ones, second)
        part_out[pl.ds(level_ref[0], 1), :] += rows[0:1, :]

    for n, (at, k) in enumerate(items):

        @pl.when(level_ref[at] >= 0)
        def _(n=n, at=at, k=k):
            for t in range(TILES):
                where = slice(k * size + t * tile, k * size + (t + 1) * tile)
                part_out[pl.ds(level_ref[at], 1), where] += jnp.sum(col_ref[(k if own else n) * TILES + t], axis=0, keepdims=True)

    if own:
        begin, end = items[0][1] * size, (items[-1][1] + 1) * size
        high_out[...] = high_ref[begin:end, :]
        low_out[...] = low_ref[begin:end, :]


def last_body(levels, owners, mass_ref, q_ref, score_ref):
    mass = mass_ref[0:owners, :]
    for z in range(1, levels):
        mass = mass + mass_ref[z * owners : (z + 1) * owners, :]
    cap = mass.shape[1]
    owner = q_ref[0:1, :]
    rank = q_ref[1:2, :]
    rows = owner.shape[1]
    at_rank = hot(iota((cap, rows), 0) == rank)
    first = mass.astype(jnp.bfloat16)
    rest = mass - first.astype(jnp.float32)
    second, third = halves(rest)
    value = mm(first, at_rank) + mm(second, at_rank) + mm(third, at_rank)
    mine = iota((owners, rows), 0) == owner
    total = jnp.sum(jnp.where(mine, value, 0.0), axis=0, keepdims=True)
    score_ref[...] = jnp.log(total * math.exp(-SHARPNESS)).reshape(rows)


def body(embeddings, cluster_ids, owner_map, source_order):
    rows, width = embeddings.shape
    clusters = owner_map.shape[0]
    levels = lax.axis_size("outer")
    inner = lax.axis_size("inner")
    groups = lax.axis_size("grp")
    owners = levels * inner
    held = clusters // owners
    cap = 2 * rows // owners
    per = cap // CHUNKS
    size = owners * per
    slots = CHUNKS * size
    share = held // (CHUNKS - 1)
    bf, i32 = jnp.bfloat16, jnp.int32
    dealt = out((owners, per + share, width))

    first, high, low, info = call(
        functools.partial(front_body, owners, per, cap),
        (dealt, out((rows, width), bf), out((rows, width), bf), out((8, rows), i32)),
        embeddings, cluster_ids, owner_map, micros=5,
    )
    back = call(
        functools.partial(back_body, owners, per, CHUNKS, held),
        (dealt,) * (CHUNKS - 1) + (out((8, rows), i32),),
        high, low, info, source_order, micros=6,
    )
    sends = (first,) + tuple(back[: CHUNKS - 1])
    q_info = back[CHUNKS - 1]
    tile = size // TILES
    strip = per // TILES
    blocks = slots // tile

    got, mine = [], []
    for k in range(CHUNKS):
        send = sends[k] if k == 0 else lax.optimization_barrier((sends[k], mine[-1]))[0]
        got.append(lax.all_to_all(send, PLANE, 0, 0, tiled=True))
        mine.append(got[k][:, :per, :].reshape(size, width))
    own_ids = got[0][:, per, :cap].reshape(owners, cap)
    piece = jnp.concatenate([jnp.sum(got[k][:, per:, :], axis=0) for k in range(1, CHUNKS)], axis=0)

    level = lax.axis_index("outer")
    down = lax.axis_index("inner") % 2
    seat = jnp.where(down == 1, levels - 1 - level, level)

    def pairs(moves):
        found = []
        for lane in range(inner):
            for a, b in moves:
                if lane % 2:
                    a, b = levels - 1 - a, levels - 1 - b
                found.append((a * inner + lane, b * inner + lane))
        return found

    top = levels - 1
    moves = []
    for s in range(1, top + 1):
        moves.append([(a, a + 1) for a in range(s - 1, top) if not (s == 1 and a == top - 1)])
    back_move = [(top, top - 1)]

    arrived = {}

    def direct(steps):
        return [(a, a + steps) for a in range(top + 1 - steps) if not (steps == 1 and a == top - 1)]

    ids_of = [own_ids]
    for s in range(1, top + 1):
        ids_of.append(lax.ppermute(own_ids, LINE, pairs(direct(s))))
    ids_of.insert(2, lax.ppermute(own_ids, LINE, pairs(back_move)))
    for k in range(CHUNKS):
        value = mine[k]
        for s in range(1, top + 1):
            value = lax.ppermute(value, LINE, pairs(moves[s - 1]))
            arrived[s, k] = value
        arrived["b", k] = lax.ppermute(mine[k], LINE, pairs(back_move))

    def mark(value, through):
        vm = pl.BlockSpec(memory_space=VMEM)
        return pl.pallas_call(
            tick_body, out_shape=out(through.shape), in_specs=[pl.BlockSpec(memory_space=pl.ANY), vm], out_specs=vm
        )(value, through)

    ids_of[0] = mark(arrived[1, 0], own_ids)
    keys_held = len(ids_of)
    ids, flags = call(
        functools.partial(meta_body, owners, CHUNKS),
        (out((keys_held, blocks, 1, tile)), out((8, LANES), i32)),
        *ids_of, micros=3,
    )
    keys = [1, "b"] + list(range(2, top + 1))

    def source_seat(key):
        if key == "b":
            return jnp.where(seat == top - 1, top, -1)
        got = seat >= key
        if key == 1:
            got = got & (seat < top)
        return jnp.where(got, seat - key, -1)

    seats = [seat] + [source_seat(key) for key in keys]
    level_of = jnp.stack([jnp.where(a < 0, -1, jnp.where(down == 1, top - a, a)) for a in seats]).astype(i32)
    part = jnp.zeros((levels, slots), jnp.float32)

    def gram(part, items, held, micros):
        own = items[0][0] == "own"
        visitors = [mine[k] if key == "own" else arrived[key, k] for key, k in items]
        at = tuple((0 if key == "own" else 1 + keys.index(key), k) for key, k in items)
        count = len(items)
        vm = pl.BlockSpec(memory_space=VMEM)
        any_ = pl.BlockSpec(memory_space=pl.ANY)
        own_out = ()
        if own:
            own_out = (out((count * size, width), bf),) * 2 + ((out((slots, LANES)),) if not held else ())
        scratch = [
            VMEM((slots, LANES), jnp.float32),
            VMEM((count, size, width), jnp.float32),
            VMEM((blocks if own else count * TILES, 8, tile), jnp.float32),
            pltpu.SMEM((6, count * TILES * blocks + 1), i32),
            pltpu.SemaphoreType.DMA((count,)),
            VMEM((slots, width), bf),
            VMEM((slots, width), bf),
            VMEM((slots, LANES), jnp.float32),
        ]
        if not own:
            scratch += [VMEM((count * size, width), bf)] * 2
        scratch += [pltpu.SemaphoreType.DMA((5,))]
        return pl.pallas_call(
            functools.partial(gram_body, owners, at, own, len(held)),
            out_shape=(out((levels, slots)),) + own_out,
            in_specs=[pl.BlockSpec(memory_space=pltpu.SMEM)] * 2 + [any_] * (count + len(held)) + [vm] * 2,
            out_specs=(vm,) * (1 + len(own_out)),
            scratch_shapes=scratch,
            cost_estimate=cost(micros),
            name="gram",
        )(level_of, flags, *visitors, *held, ids, part)

    plan = [
        ([("own", k) for k in range(CHUNKS)], 13),
        ([(1, 0), ("b", 0), (2, 0)], 14),
        ([(1, 1), ("b", 1), (2, 1)], 14),
        ([(1, 2), ("b", 2), (2, 2), (3, 0)], 17),
        ([(3, 1)], 8),
        ([(3, 2)], 8),
    ]
    held_here = ()
    for items, micros in plan:
        part, *made = gram(part, items, held_here, micros)
        held_here += tuple(made)
    total = None
    for s in range(groups):
        route = [(g * levels + z, ((z + s) % groups) * levels + g) for g in range(groups) for z in range(levels)]
        came = lax.ppermute(piece, ("grp", "outer"), route)
        total = came if total is None else total + came
    centroids = total * lax.rsqrt(jnp.mean(total * total, axis=1, keepdims=True) + 1e-6)
    parts = part.reshape(levels, CHUNKS, TILES, owners, strip).transpose(0, 3, 1, 2, 4).reshape(levels * owners, cap)
    home = lax.all_to_all(parts, BY_LEVEL, 0, 0, tiled=True)
    score = call(functools.partial(last_body, levels, owners), out((rows,)), home, q_info, micros=2)

    return score, centroids


def solution(mesh):
    groups, owned = mesh.shape["grp"], mesh.shape["own"]
    split = Mesh(mesh.devices.reshape(groups, groups, owned // groups), EVERY)
    return jax.shard_map(
        body,
        mesh=split,
        in_specs=(P(EVERY, None), P(EVERY), P(), P(EVERY)),
        out_specs=(P(EVERY), P(LINE, None)),
        check_vma=False,
    )
```

```python
import functools
import math

import jax
import jax.numpy as jnp
from jax import lax
from jax.experimental import pallas as pl
from jax.experimental.pallas import tpu as pltpu
from jax.sharding import Mesh
from jax.sharding import PartitionSpec as P


SHARPNESS = 6.0
SCALE = (SHARPNESS * 1.4426950408889634) ** 0.5
CHUNKS = 3
TILES = 2
LANES = 128
VMEM = pltpu.VMEM
EVERY = ("grp", "outer", "inner")
PLANE = ("grp", "inner")
LINE = ("outer", "inner")
BY_LEVEL = ("outer", "grp", "inner")
NT = (((1,), (1,)), ((), ()))


def iota(shape, axis):
    return lax.broadcasted_iota(jnp.int32, shape, axis)


def mm(left, right):
    return jnp.dot(left, right, preferred_element_type=jnp.float32)


def mm_nt(left, right):
    return lax.dot_general(left, right, NT, preferred_element_type=jnp.float32)


def halves(value):
    high = value.astype(jnp.bfloat16)
    low = (value - high.astype(jnp.float32)).astype(jnp.bfloat16)
    return high, low


def hot(mask):
    return jnp.where(mask, 1.0, 0.0).astype(jnp.bfloat16)


def cost(micros):
    return pl.CostEstimate(flops=int(micros * 1.1e9), transcendentals=0, bytes_accessed=0)


def call(body, outs, *args, micros, scratch=(), smem=0, aliases=None):
    spec = [pl.BlockSpec(memory_space=pltpu.SMEM)] * smem
    spec += [pl.BlockSpec(memory_space=VMEM)] * (len(args) - smem)
    return pl.pallas_call(
        body,
        out_shape=outs,
        in_specs=spec,
        out_specs=jax.tree.map(lambda _: pl.BlockSpec(memory_space=VMEM), outs),
        scratch_shapes=list(scratch),
        input_output_aliases=aliases or {},
        cost_estimate=cost(micros),
    )(*args)


def out(shape, dtype=jnp.float32):
    return jax.ShapeDtypeStruct(shape, dtype)


def chunk_rows(owner, rank, high, low, k, owners, per):
    inside = (rank >= k * per) & (rank < (k + 1) * per)
    dest = jnp.where(inside, owner * per + rank - k * per, -1)
    pick = hot(iota((owners * per, dest.shape[1]), 0) == dest)
    return mm(pick, high) + mm(pick, low)


def front_body(owners, per, cap, x_ref, ids_ref, om_ref, chunk_ref, high_ref, low_ref, info_ref):
    x = x_ref[...]
    rows, width = x.shape
    clusters = om_ref.shape[0]
    ids = ids_ref[...].reshape(1, rows)
    square = (clusters, clusters)
    om_row = jnp.broadcast_to(om_ref[...].reshape(1, clusters), square)
    om_col = jnp.transpose(om_row.astype(jnp.float32)).astype(jnp.int32)
    om = om_col[:, 0:1]
    here = iota((clusters, rows), 0) == ids
    owner = jnp.sum(jnp.where(here, om, 0), axis=0, keepdims=True)
    mine = iota((owners, rows), 0) == owner
    member = hot(here)
    within = mm(member, hot(iota((rows, rows), 0) < iota((rows, rows), 1)))
    earlier = (om_col == om_row) & (iota(square, 1) < iota(square, 0))
    base = jnp.sum(mm(hot(earlier), member), axis=1, keepdims=True)
    rank = jnp.sum(jnp.where(here, within + base, 0.0), axis=0, keepdims=True)
    count = jnp.sum(mine.astype(jnp.float32), axis=1, keepdims=True)
    count = jnp.sum(jnp.where(mine, count, 0.0), axis=0, keepdims=True)
    rank = jnp.floor((rank * cap + 0.5) / count).astype(jnp.int32)
    order = om * (clusters // owners) + jnp.sum(earlier.astype(jnp.int32), axis=1, keepdims=True)
    position = jnp.sum(jnp.where(here, order, 0), axis=0, keepdims=True)
    info_ref[...] = jnp.concatenate([owner, rank, position, position] * 2, axis=0)
    unit = x * lax.rsqrt(jnp.sum(x * x, axis=1, keepdims=True) + 1e-6)
    high, low = halves(unit)
    high_ref[...] = high
    low_ref[...] = low
    chunk_ref[:, 0:per, :] = chunk_rows(owner, rank, high, low, 0, owners, per).reshape(owners, per, width)
    at_rank = hot(iota((cap, rows), 0) == rank)
    coarse = (ids + 1) // 16
    fine = ids + 1 - coarse * 16
    coarse = jnp.where(mine, coarse.astype(jnp.float32), 0.0).astype(jnp.bfloat16)
    fine = jnp.where(mine, fine.astype(jnp.float32), 0.0).astype(jnp.bfloat16)
    sid = mm_nt(coarse, at_rank) * 16.0 + mm_nt(fine, at_rank) - 1.0
    for p in range(owners):
        chunk_ref[p, per:, :] = jnp.zeros(chunk_ref[p, per:, :].shape, jnp.float32)
        chunk_ref[p, per : per + 1, 0:cap] = sid[p : p + 1, :]


def back_body(owners, per, chunks, held, high_ref, low_ref, info_ref, so_ref, *outs):
    high = high_ref[...]
    low = low_ref[...]
    owner = info_ref[0:1, :]
    rank = info_ref[1:2, :]
    position = info_ref[2:3, :]
    rows, width = high.shape
    clusters = owners * held
    pick = hot(iota((clusters, rows), 0) == position)
    sums = (mm(pick, high) + mm(pick, low)).reshape(owners, held, width)
    for k in range(1, chunks):
        outs[k - 1][:, 0:per, :] = chunk_rows(owner, rank, high, low, k, owners, per).reshape(owners, per, width)
    outs[0][:, per:, :] = sums
    q_ref = outs[chunks - 1]
    target = hot(iota((rows, rows), 0) == so_ref[...].reshape(1, rows))
    values = info_ref[...].astype(jnp.float32).astype(jnp.bfloat16)
    q_ref[...] = mm_nt(values, target).astype(jnp.int32)


def by_tile(owners, value_ref, high_ref, low_ref, start):
    size = value_ref.shape[0]
    per = size // owners
    strip = per // TILES
    for t in range(TILES):
        for p in range(owners):
            rows = value_ref[p * per + t * strip : p * per + (t + 1) * strip, :]
            high, low = halves(rows * SCALE)
            to = start + (t * owners + p) * strip
            high_ref[to : to + strip, :] = high
            low_ref[to : to + strip, :] = low


def tick_body(value_ref, through_ref, out_ref):
    out_ref[...] = through_ref[...]


def meta_body(owners, chunks, *refs):
    count = len(refs) - 2
    ids_out, flag_out = refs[count:]
    cap = refs[0].shape[1]
    blocks = chunks * TILES
    tile = ids_out.shape[3]
    strip = cap // blocks
    slots = blocks * tile
    ids = jnp.concatenate([ref[...] for ref in refs[:count]], axis=0)
    coarse = jnp.floor(ids * 0.0625)
    fine = ids - coarse * 16.0
    lane = iota((cap, slots), 1)
    spread = hot(iota((cap, slots), 0) == lane // tile * strip + lane % strip)
    wide = mm(coarse.astype(jnp.bfloat16), spread) * 16.0 + mm(fine.astype(jnp.bfloat16), spread)
    sender = iota((owners, slots), 1) % tile // strip == iota((owners, slots), 0)
    flag_lane = iota((1, LANES), 1)
    ends = []
    for key in range(count):
        row = jnp.sum(jnp.where(sender, wide[key * owners : (key + 1) * owners, :], 0.0), axis=0, keepdims=True)
        found = []
        for t in range(blocks):
            part = row[:, t * tile : (t + 1) * tile]
            ids_out[key, t] = part
            least = jnp.min(jnp.where(part < 0.0, 1e6, part), axis=1, keepdims=True)
            found.append((least, jnp.max(part, axis=1, keepdims=True)))
        ends.append(found)
        flags = jnp.zeros((1, LANES), jnp.int32)
        for t in range(blocks):
            for b in range(blocks):
                met = (found[t][0] <= ends[0][b][1]) & (ends[0][b][0] <= found[t][1])
                flags = jnp.where((flag_lane == t * blocks + b) & met, 1, flags)
        flag_out[key : key + 1, :] = flags
    flag_out[count:, :] = jnp.zeros((flag_out.shape[0] - count, LANES), jnp.int32)


def gram_body(owners, items, own, held, level_ref, flag_ref, *refs):
    count = len(items)
    visitors = refs[:count]
    refs = refs[count:]
    kept = refs[:held]
    refs = refs[held:]
    if own:
        ids_ref, part_ref, part_out, high_out, low_out, lid_out = refs[:6] if held == 0 else refs[:5] + (None,)
        refs = refs[6 if held == 0 else 5 :]
    else:
        ids_ref, part_ref, part_out = refs[:3]
        refs = refs[3:]
    acc_ref, v_ref, col_ref, pair_ref, sem, high_ref, low_ref, lid_ref = refs[:8]
    if own:
        vh_ref, vl_ref = high_ref, low_ref
        own_sem = refs[8]
    else:
        vh_ref, vl_ref, own_sem = refs[8:]
    size = v_ref.shape[1]
    slots = high_ref.shape[0]
    tile = size // TILES
    blocks = slots // tile
    part_out[...] = part_ref[...]
    alive = level_ref[items[0][0]] >= 0
    for at, k in items[1:]:
        alive = alive | (level_ref[at] >= 0)

    def fetch(n):
        return pltpu.make_async_copy(visitors[n], v_ref.at[n], sem.at[n])

    for n, (at, k) in enumerate(items):

        @pl.when(level_ref[at] >= 0)
        def _(n=n):
            fetch(n).start()

    copies = []
    if held:
        early = kept[0].shape[0]
        places = [(kept[0], high_ref.at[0:early]), (kept[1], low_ref.at[0:early]), (kept[2], lid_ref)]
        if held > 3:
            places += [(kept[3], high_ref.at[early:slots]), (kept[4], low_ref.at[early:slots])]
        copies = [pltpu.make_async_copy(*place, own_sem.at[n]) for n, place in enumerate(places)]

    @pl.when(alive)
    def _():
        for copy in copies:
            copy.start()
        acc_ref[...] = jnp.zeros_like(acc_ref)
        col_ref[...] = jnp.zeros_like(col_ref)
        if own and held == 0:
            for b in range(slots // LANES):
                row = ids_ref[0, b * LANES // tile, :, b * LANES % tile : b * LANES % tile + LANES]
                lid_ref[b * LANES : (b + 1) * LANES, :] = jnp.transpose(jnp.broadcast_to(row, (LANES, LANES)))
            lid_out[...] = lid_ref[...]

    total = jnp.int32(0)
    for n, (at, k) in enumerate(items):
        live = level_ref[at] >= 0
        for t in range(TILES):
            begin, end = jnp.int32(blocks), jnp.int32(-1)
            for b in range(blocks):
                met = flag_ref[at, (k * TILES + t) * blocks + b] > 0
                if own and b > k * TILES + t:
                    continue
                begin = jnp.where(met, jnp.minimum(begin, b), begin)
                end = jnp.where(met, b, end)
            for w in range((blocks + 1) // 2):
                start = begin + 2 * w
                used = jnp.minimum(start, blocks - 2)
                pair_ref[0, total] = used
                pair_ref[1, total] = (k if own else n) * TILES + t
                pair_ref[2, total] = k * TILES + t
                pair_ref[3, total] = at
                pair_ref[4, total] = (used == start).astype(jnp.int32)
                pair_ref[5, total] = (used < end).astype(jnp.int32)
                total = total + (live & (start <= end)).astype(jnp.int32)

    for n, (at, k) in enumerate(items):

        @pl.when(level_ref[at] >= 0)
        def _(n=n):
            fetch(n).wait()
            by_tile(owners, v_ref.at[n], vh_ref, vl_ref, (items[n][1] if own else n) * size)

    @pl.when(alive)
    def _():
        for copy in copies:
            copy.wait()

        def step(i, _):
            b = pair_ref[0, i]
            v = pair_ref[1, i]
            vid = ids_ref[pair_ref[3, i], pair_ref[2, i]]
            rows = pl.ds(pl.multiple_of(b * tile, tile), 2 * tile)
            cols = pl.ds(pl.multiple_of(v * tile, tile), tile)
            left_h = high_ref[rows, :]
            right_h = vh_ref[cols, :]
            left = jnp.concatenate([left_h, left_h, low_ref[rows, :]], axis=1)
            right = jnp.concatenate([right_h, vl_ref[cols, :], right_h], axis=1)
            score = mm_nt(left, right)
            for h in range(2):
                half = pl.ds(pl.multiple_of((b + h) * tile, tile), tile)
                lid = lid_ref[half, :]
                row_part = acc_ref[half, :]
                wanted = vid + jnp.where(pair_ref[4 + h, i] > 0, 0.0, 1e6)
                for c in range(tile // LANES):
                    lanes = slice(c * LANES, (c + 1) * LANES)
                    weight = jnp.exp2(score[h * tile : (h + 1) * tile, lanes])
                    weight = jnp.where(lid == wanted[:, lanes], weight, 0.0)
                    row_part = row_part + weight
                    col = jnp.sum(weight.reshape(tile // 8, 8, LANES), axis=0)
                    col_ref[v, :, lanes] += col * jnp.where(b + h < v, 1.0, 0.0) if own else col
                acc_ref[half, :] = row_part
            return 0

        lax.fori_loop(0, total, step, 0)
        first, rest = halves(acc_ref[...])
        second, _ = halves(acc_ref[...] - first.astype(jnp.float32) - rest.astype(jnp.float32))
        ones = jnp.ones((8, LANES), jnp.bfloat16)
        rows = mm_nt(ones, first) + mm_nt(ones, rest) + mm_nt(ones, second)
        part_out[pl.ds(level_ref[0], 1), :] += rows[0:1, :]

    for n, (at, k) in enumerate(items):

        @pl.when(level_ref[at] >= 0)
        def _(n=n, at=at, k=k):
            for t in range(TILES):
                where = slice(k * size + t * tile, k * size + (t + 1) * tile)
                part_out[pl.ds(level_ref[at], 1), where] += jnp.sum(col_ref[(k if own else n) * TILES + t], axis=0, keepdims=True)

    if own:
        begin, end = items[0][1] * size, (items[-1][1] + 1) * size
        high_out[...] = high_ref[begin:end, :]
        low_out[...] = low_ref[begin:end, :]


def last_body(levels, owners, mass_ref, q_ref, score_ref):
    mass = mass_ref[0:owners, :]
    for z in range(1, levels):
        mass = mass + mass_ref[z * owners : (z + 1) * owners, :]
    cap = mass.shape[1]
    owner = q_ref[0:1, :]
    rank = q_ref[1:2, :]
    rows = owner.shape[1]
    at_rank = hot(iota((cap, rows), 0) == rank)
    first = mass.astype(jnp.bfloat16)
    rest = mass - first.astype(jnp.float32)
    second, third = halves(rest)
    value = mm(first, at_rank) + mm(second, at_rank) + mm(third, at_rank)
    mine = iota((owners, rows), 0) == owner
    total = jnp.sum(jnp.where(mine, value, 0.0), axis=0, keepdims=True)
    score_ref[...] = jnp.log(total * math.exp(-SHARPNESS)).reshape(rows)


def body(embeddings, cluster_ids, owner_map, source_order):
    rows, width = embeddings.shape
    clusters = owner_map.shape[0]
    levels = lax.axis_size("outer")
    inner = lax.axis_size("inner")
    groups = lax.axis_size("grp")
    owners = levels * inner
    held = clusters // owners
    cap = 2 * rows // owners
    per = cap // CHUNKS
    size = owners * per
    slots = CHUNKS * size
    bf, i32 = jnp.bfloat16, jnp.int32
    dealt = [out((owners, per + extra, width)) for extra in (8, held, 0)]

    first, high, low, info = call(
        functools.partial(front_body, owners, per, cap),
        (dealt[0], out((rows, width), bf), out((rows, width), bf), out((8, rows), i32)),
        embeddings, cluster_ids, owner_map, micros=5,
    )
    back = call(
        functools.partial(back_body, owners, per, CHUNKS, held),
        tuple(dealt[1:]) + (out((8, rows), i32),),
        high, low, info, source_order, micros=6,
    )
    sends = (first,) + tuple(back[: CHUNKS - 1])
    q_info = back[CHUNKS - 1]
    tile = size // TILES
    strip = per // TILES
    blocks = slots // tile

    got, mine = [], []
    for k in range(CHUNKS):
        send = sends[k] if k == 0 else lax.optimization_barrier((sends[k], mine[-1]))[0]
        got.append(lax.all_to_all(send, PLANE, 0, 0, tiled=True))
        mine.append(got[k][:, :per, :].reshape(size, width))
    own_ids = got[0][:, per, :cap].reshape(owners, cap)
    piece = jnp.sum(got[1][:, per:, :], axis=0)

    level = lax.axis_index("outer")
    down = lax.axis_index("inner") % 2
    seat = jnp.where(down == 1, levels - 1 - level, level)

    def pairs(moves):
        found = []
        for lane in range(inner):
            for a, b in moves:
                if lane % 2:
                    a, b = levels - 1 - a, levels - 1 - b
                found.append((a * inner + lane, b * inner + lane))
        return found

    top = levels - 1
    moves = []
    for s in range(1, top + 1):
        moves.append([(a, a + 1) for a in range(s - 1, top) if not (s == 1 and a == top - 1)])
    back_move = [(top, top - 1)]

    arrived = {}

    def direct(steps):
        return [(a, a + steps) for a in range(top + 1 - steps) if not (steps == 1 and a == top - 1)]

    ids_of = [own_ids]
    for s in range(1, top + 1):
        ids_of.append(lax.ppermute(own_ids, LINE, pairs(direct(s))))
    ids_of.insert(2, lax.ppermute(own_ids, LINE, pairs(back_move)))
    for k in range(CHUNKS):
        value = mine[k]
        for s in range(1, top + 1):
            value = lax.ppermute(value, LINE, pairs(moves[s - 1]))
            arrived[s, k] = value
        arrived["b", k] = lax.ppermute(mine[k], LINE, pairs(back_move))

    def mark(value, through):
        vm = pl.BlockSpec(memory_space=VMEM)
        return pl.pallas_call(
            tick_body, out_shape=out(through.shape), in_specs=[pl.BlockSpec(memory_space=pl.ANY), vm], out_specs=vm
        )(value, through)

    ids_of[0] = mark(arrived[1, 0], own_ids)
    keys_held = len(ids_of)
    ids, flags = call(
        functools.partial(meta_body, owners, CHUNKS),
        (out((keys_held, blocks, 1, tile)), out((8, LANES), i32)),
        *ids_of, micros=3,
    )
    keys = [1, "b"] + list(range(2, top + 1))

    def source_seat(key):
        if key == "b":
            return jnp.where(seat == top - 1, top, -1)
        got = seat >= key
        if key == 1:
            got = got & (seat < top)
        return jnp.where(got, seat - key, -1)

    seats = [seat] + [source_seat(key) for key in keys]
    level_of = jnp.stack([jnp.where(a < 0, -1, jnp.where(down == 1, top - a, a)) for a in seats]).astype(i32)
    part = jnp.zeros((levels, slots), jnp.float32)

    def gram(part, items, held, micros):
        own = items[0][0] == "own"
        visitors = [mine[k] if key == "own" else arrived[key, k] for key, k in items]
        at = tuple((0 if key == "own" else 1 + keys.index(key), k) for key, k in items)
        count = len(items)
        vm = pl.BlockSpec(memory_space=VMEM)
        any_ = pl.BlockSpec(memory_space=pl.ANY)
        own_out = ()
        if own:
            own_out = (out((count * size, width), bf),) * 2 + ((out((slots, LANES)),) if not held else ())
        scratch = [
            VMEM((slots, LANES), jnp.float32),
            VMEM((count, size, width), jnp.float32),
            VMEM((blocks if own else count * TILES, 8, tile), jnp.float32),
            pltpu.SMEM((6, count * TILES * blocks + 1), i32),
            pltpu.SemaphoreType.DMA((count,)),
            VMEM((slots, width), bf),
            VMEM((slots, width), bf),
            VMEM((slots, LANES), jnp.float32),
        ]
        if not own:
            scratch += [VMEM((count * size, width), bf)] * 2
        scratch += [pltpu.SemaphoreType.DMA((5,))]
        return pl.pallas_call(
            functools.partial(gram_body, owners, at, own, len(held)),
            out_shape=(out((levels, slots)),) + own_out,
            in_specs=[pl.BlockSpec(memory_space=pltpu.SMEM)] * 2 + [any_] * (count + len(held)) + [vm] * 2,
            out_specs=(vm,) * (1 + len(own_out)),
            scratch_shapes=scratch,
            cost_estimate=cost(micros),
            name="gram",
        )(level_of, flags, *visitors, *held, ids, part)

    plan = [
        ([("own", k) for k in range(CHUNKS)], 13),
        ([(1, 0), ("b", 0), (2, 0)], 14),
        ([(1, 1), ("b", 1)], 11),
        ([(2, 1), (1, 2), (2, 2), (3, 0)], 17),
        ([(3, 1)], 8),
        ([("b", 2), (3, 2)], 8),
    ]
    held_here = ()
    for items, micros in plan:
        part, *made = gram(part, items, held_here, micros)
        held_here += tuple(made)
    total = None
    for s in range(groups):
        route = [(g * levels + z, ((z + s) % groups) * levels + g) for g in range(groups) for z in range(levels)]
        came = lax.ppermute(piece, ("grp", "outer"), route)
        total = came if total is None else total + came
    centroids = total * lax.rsqrt(jnp.mean(total * total, axis=1, keepdims=True) + 1e-6)
    parts = part.reshape(levels, CHUNKS, TILES, owners, strip).transpose(0, 3, 1, 2, 4).reshape(levels * owners, cap)
    home = lax.all_to_all(parts, BY_LEVEL, 0, 0, tiled=True)
    score = call(functools.partial(last_body, levels, owners), out((rows,)), home, q_info, micros=2)

    return score, centroids


def solution(mesh):
    groups, owned = mesh.shape["grp"], mesh.shape["own"]
    split = Mesh(mesh.devices.reshape(groups, groups, owned // groups), EVERY)
    return jax.shard_map(
        body,
        mesh=split,
        in_specs=(P(EVERY, None), P(EVERY), P(), P(EVERY)),
        out_specs=(P(EVERY), P(LINE, None)),
        check_vma=False,
    )
```

```python
import functools
import math

import jax
import jax.numpy as jnp
from jax import lax
from jax.experimental import pallas as pl
from jax.experimental.pallas import tpu as pltpu
from jax.sharding import Mesh
from jax.sharding import PartitionSpec as P


SHARPNESS = 6.0
SCALE = (SHARPNESS * 1.4426950408889634) ** 0.5
CHUNKS = 3
TILES = 2
LANES = 128
VMEM = pltpu.VMEM
EVERY = ("grp", "outer", "inner")
PLANE = ("grp", "inner")
LINE = ("outer", "inner")
BY_LEVEL = ("outer", "grp", "inner")
NT = (((1,), (1,)), ((), ()))


def iota(shape, axis):
    return lax.broadcasted_iota(jnp.int32, shape, axis)


def mm(left, right):
    return jnp.dot(left, right, preferred_element_type=jnp.float32)


def mm_nt(left, right):
    return lax.dot_general(left, right, NT, preferred_element_type=jnp.float32)


def halves(value):
    high = value.astype(jnp.bfloat16)
    low = (value - high.astype(jnp.float32)).astype(jnp.bfloat16)
    return high, low


def hot(mask):
    return jnp.where(mask, 1.0, 0.0).astype(jnp.bfloat16)


def cost(micros):
    return pl.CostEstimate(flops=int(micros * 1.1e9), transcendentals=0, bytes_accessed=0)


def call(body, outs, *args, micros, scratch=(), smem=0, aliases=None):
    spec = [pl.BlockSpec(memory_space=pltpu.SMEM)] * smem
    spec += [pl.BlockSpec(memory_space=VMEM)] * (len(args) - smem)
    return pl.pallas_call(
        body,
        out_shape=outs,
        in_specs=spec,
        out_specs=jax.tree.map(lambda _: pl.BlockSpec(memory_space=VMEM), outs),
        scratch_shapes=list(scratch),
        input_output_aliases=aliases or {},
        cost_estimate=cost(micros),
    )(*args)


def out(shape, dtype=jnp.float32):
    return jax.ShapeDtypeStruct(shape, dtype)


def unit_halves(x):
    return halves(x * lax.rsqrt(jnp.sum(x * x, axis=1, keepdims=True) + 1e-6))


def chunk_rows(owner, rank, high, low, k, owners, per):
    inside = (rank >= k * per) & (rank < (k + 1) * per)
    dest = jnp.where(inside, owner * per + rank - k * per, -1)
    pick = hot(iota((owners * per, dest.shape[1]), 0) == dest)
    return mm(pick, high) + mm(pick, low)


def front_body(owners, per, cap, x_ref, ids_ref, om_ref, chunk_ref, info_ref):
    x = x_ref[...]
    rows, width = x.shape
    clusters = om_ref.shape[0]
    ids = ids_ref[...].reshape(1, rows)
    square = (clusters, clusters)
    om_row = jnp.broadcast_to(om_ref[...].reshape(1, clusters), square)
    om_col = jnp.transpose(om_row.astype(jnp.float32)).astype(jnp.int32)
    om = om_col[:, 0:1]
    here = iota((clusters, rows), 0) == ids
    owner = jnp.sum(jnp.where(here, om, 0), axis=0, keepdims=True)
    mine = iota((owners, rows), 0) == owner
    member = hot(here)
    step = LANES if rows % LANES == 0 else rows
    ahead = hot(iota((step, step), 0) < iota((step, step), 1))
    every = jnp.ones((step, step), jnp.bfloat16)
    seen, within = jnp.zeros((clusters, step), jnp.float32), []
    for b in range(0, rows, step):
        part = member[:, b : b + step]
        within.append(mm(part, ahead) + seen)
        seen = seen + mm(part, every)
    within = jnp.concatenate(within, axis=1)
    earlier = (om_col == om_row) & (iota(square, 1) < iota(square, 0))
    base = jnp.sum(mm(hot(earlier), member), axis=1, keepdims=True)
    rank = jnp.sum(jnp.where(here, within + base, 0.0), axis=0, keepdims=True)
    count = jnp.sum(mine.astype(jnp.float32), axis=1, keepdims=True)
    count = jnp.sum(jnp.where(mine, count, 0.0), axis=0, keepdims=True)
    rank = jnp.floor((rank * cap + 0.5) / count).astype(jnp.int32)
    order = om * (clusters // owners) + jnp.sum(earlier.astype(jnp.int32), axis=1, keepdims=True)
    position = jnp.sum(jnp.where(here, order, 0), axis=0, keepdims=True)
    info_ref[...] = jnp.concatenate([owner, rank, position, position] * 2, axis=0)
    high, low = unit_halves(x)
    chunk_ref[:, 0:per, :] = chunk_rows(owner, rank, high, low, 0, owners, per).reshape(owners, per, width)
    at_rank = hot(iota((cap, rows), 0) == rank)
    coarse = (ids + 1) // 16
    fine = ids + 1 - coarse * 16
    coarse = jnp.where(mine, coarse.astype(jnp.float32), 0.0).astype(jnp.bfloat16)
    fine = jnp.where(mine, fine.astype(jnp.float32), 0.0).astype(jnp.bfloat16)
    sid = mm_nt(coarse, at_rank) * 16.0 + mm_nt(fine, at_rank) - 1.0
    for p in range(owners):
        chunk_ref[p, per:, :] = jnp.zeros(chunk_ref[p, per:, :].shape, jnp.float32)
        chunk_ref[p, per : per + 1, 0:cap] = sid[p : p + 1, :]


def back_body(owners, per, chunks, held, x_ref, info_ref, so_ref, *outs):
    high, low = unit_halves(x_ref[...])
    owner = info_ref[0:1, :]
    rank = info_ref[1:2, :]
    position = info_ref[2:3, :]
    rows, width = high.shape
    clusters = owners * held
    pick = hot(iota((clusters, rows), 0) == position)
    sums = (mm(pick, high) + mm(pick, low)).reshape(owners, held, width)
    for k in range(1, chunks):
        outs[k - 1][:, 0:per, :] = chunk_rows(owner, rank, high, low, k, owners, per).reshape(owners, per, width)
    outs[0][:, per:, :] = sums
    q_ref = outs[chunks - 1]
    target = hot(iota((rows, rows), 0) == so_ref[...].reshape(1, rows))
    values = info_ref[...].astype(jnp.float32).astype(jnp.bfloat16)
    q_ref[...] = mm_nt(values, target).astype(jnp.int32)


def by_tile(owners, value_ref, high_ref, low_ref, start):
    size = value_ref.shape[0]
    per = size // owners
    strip = per // TILES
    for t in range(TILES):
        for p in range(owners):
            rows = value_ref[p * per + t * strip : p * per + (t + 1) * strip, :]
            high, low = halves(rows * SCALE)
            to = start + (t * owners + p) * strip
            high_ref[to : to + strip, :] = high
            low_ref[to : to + strip, :] = low


def tick_body(value_ref, through_ref, out_ref):
    out_ref[...] = through_ref[...]


def meta_body(owners, chunks, *refs):
    count = len(refs) - 2
    ids_out, flag_out = refs[count:]
    cap = refs[0].shape[1]
    blocks = chunks * TILES
    tile = ids_out.shape[3]
    strip = cap // blocks
    slots = blocks * tile
    ids = jnp.concatenate([ref[...] for ref in refs[:count]], axis=0)
    coarse = jnp.floor(ids * 0.0625)
    fine = ids - coarse * 16.0
    lane = iota((cap, slots), 1)
    spread = hot(iota((cap, slots), 0) == lane // tile * strip + lane % strip)
    wide = mm(coarse.astype(jnp.bfloat16), spread) * 16.0 + mm(fine.astype(jnp.bfloat16), spread)
    sender = iota((owners, slots), 1) % tile // strip == iota((owners, slots), 0)
    flag_lane = iota((1, LANES), 1)
    ends = []
    for key in range(count):
        row = jnp.sum(jnp.where(sender, wide[key * owners : (key + 1) * owners, :], 0.0), axis=0, keepdims=True)
        found = []
        for t in range(blocks):
            part = row[:, t * tile : (t + 1) * tile]
            ids_out[key, t] = part
            least = jnp.min(jnp.where(part < 0.0, 1e6, part), axis=1, keepdims=True)
            found.append((least, jnp.max(part, axis=1, keepdims=True)))
        ends.append(found)
        flags = jnp.zeros((1, LANES), jnp.int32)
        for t in range(blocks):
            for b in range(blocks):
                met = (found[t][0] <= ends[0][b][1]) & (ends[0][b][0] <= found[t][1])
                flags = jnp.where((flag_lane == t * blocks + b) & met, 1, flags)
        flag_out[key : key + 1, :] = flags
    flag_out[count:, :] = jnp.zeros((flag_out.shape[0] - count, LANES), jnp.int32)


def gram_body(owners, items, own, held, level_ref, flag_ref, *refs):
    count = len(items)
    visitors = refs[:count]
    refs = refs[count:]
    kept = refs[:held]
    refs = refs[held:]
    if own:
        ids_ref, part_ref, part_out, high_out, low_out, lid_out = refs[:6] if held == 0 else refs[:5] + (None,)
        refs = refs[6 if held == 0 else 5 :]
    else:
        ids_ref, part_ref, part_out = refs[:3]
        refs = refs[3:]
    acc_ref, v_ref, col_ref, pair_ref, sem, high_ref, low_ref, lid_ref = refs[:8]
    if own:
        vh_ref, vl_ref = high_ref, low_ref
        own_sem = refs[8]
    else:
        vh_ref, vl_ref, own_sem = refs[8:]
    size = v_ref.shape[1]
    slots = high_ref.shape[0]
    tile = size // TILES
    blocks = slots // tile
    sums = pltpu.make_async_copy(part_ref, part_out, own_sem.at[5])
    sums.start()
    alive = level_ref[items[0][0]] >= 0
    for at, k in items[1:]:
        alive = alive | (level_ref[at] >= 0)

    def fetch(n):
        return pltpu.make_async_copy(visitors[n], v_ref.at[n], sem.at[n])

    for n, (at, k) in enumerate(items):

        @pl.when(level_ref[at] >= 0)
        def _(n=n):
            fetch(n).start()

    copies = []
    if held:
        early = kept[0].shape[0]
        places = [(kept[0], high_ref.at[0:early]), (kept[1], low_ref.at[0:early]), (kept[2], lid_ref)]
        if held > 3:
            places += [(kept[3], high_ref.at[early:slots]), (kept[4], low_ref.at[early:slots])]
        copies = [pltpu.make_async_copy(*place, own_sem.at[n]) for n, place in enumerate(places)]

    @pl.when(alive)
    def _():
        for copy in copies:
            copy.start()
        acc_ref[...] = jnp.zeros_like(acc_ref)
        col_ref[...] = jnp.zeros_like(col_ref)
        if own and held == 0:
            for b in range(slots // LANES):
                row = ids_ref[0, b * LANES // tile, :, b * LANES % tile : b * LANES % tile + LANES]
                lid_ref[b * LANES : (b + 1) * LANES, :] = jnp.transpose(jnp.broadcast_to(row, (LANES, LANES)))
            lid_out[...] = lid_ref[...]

    total = jnp.int32(0)
    for n, (at, k) in enumerate(items):
        live = level_ref[at] >= 0
        for t in range(TILES):
            begin, end = jnp.int32(blocks), jnp.int32(-1)
            for b in range(blocks):
                met = flag_ref[at, (k * TILES + t) * blocks + b] > 0
                if own and b > k * TILES + t:
                    continue
                begin = jnp.where(met, jnp.minimum(begin, b), begin)
                end = jnp.where(met, b, end)
            for w in range((blocks + 1) // 2):
                start = begin + 2 * w
                used = jnp.minimum(start, blocks - 2)
                pair_ref[0, total] = used
                pair_ref[1, total] = (k if own else n) * TILES + t
                pair_ref[2, total] = k * TILES + t
                pair_ref[3, total] = at
                pair_ref[4, total] = (used == start).astype(jnp.int32)
                pair_ref[5, total] = (used < end).astype(jnp.int32)
                total = total + (live & (start <= end)).astype(jnp.int32)

    sums.wait()
    for n, (at, k) in enumerate(items):

        @pl.when(level_ref[at] >= 0)
        def _(n=n):
            fetch(n).wait()
            by_tile(owners, v_ref.at[n], vh_ref, vl_ref, (items[n][1] if own else n) * size)

    @pl.when(alive)
    def _():
        for copy in copies:
            copy.wait()

        def step(i, _):
            b = pair_ref[0, i]
            v = pair_ref[1, i]
            vid = ids_ref[pair_ref[3, i], pair_ref[2, i]]
            rows = pl.ds(pl.multiple_of(b * tile, tile), 2 * tile)
            cols = pl.ds(pl.multiple_of(v * tile, tile), tile)
            left_h = high_ref[rows, :]
            right_h = vh_ref[cols, :]
            left = jnp.concatenate([left_h, left_h, low_ref[rows, :]], axis=1)
            right = jnp.concatenate([right_h, vl_ref[cols, :], right_h], axis=1)
            score = mm_nt(left, right)
            for h in range(2):
                half = pl.ds(pl.multiple_of((b + h) * tile, tile), tile)
                lid = lid_ref[half, :]
                row_part = acc_ref[half, :]
                wanted = vid + jnp.where(pair_ref[4 + h, i] > 0, 0.0, 1e6)
                for c in range(tile // LANES):
                    lanes = slice(c * LANES, (c + 1) * LANES)
                    weight = jnp.exp2(score[h * tile : (h + 1) * tile, lanes])
                    weight = jnp.where(lid == wanted[:, lanes], weight, 0.0)
                    row_part = row_part + weight
                    col = jnp.sum(weight.reshape(tile // 8, 8, LANES), axis=0)
                    col_ref[v, :, lanes] += col * jnp.where(b + h < v, 1.0, 0.0) if own else col
                acc_ref[half, :] = row_part
            return 0

        lax.fori_loop(0, total, step, 0)
        first, rest = halves(acc_ref[...])
        second, _ = halves(acc_ref[...] - first.astype(jnp.float32) - rest.astype(jnp.float32))
        ones = jnp.ones((8, LANES), jnp.bfloat16)
        rows = mm_nt(ones, first) + mm_nt(ones, rest) + mm_nt(ones, second)
        part_out[pl.ds(level_ref[0], 1), :] += rows[0:1, :]

    for n, (at, k) in enumerate(items):

        @pl.when(level_ref[at] >= 0)
        def _(n=n, at=at, k=k):
            for t in range(TILES):
                where = slice(k * size + t * tile, k * size + (t + 1) * tile)
                part_out[pl.ds(level_ref[at], 1), where] += jnp.sum(col_ref[(k if own else n) * TILES + t], axis=0, keepdims=True)

    if own:
        begin, end = items[0][1] * size, (items[-1][1] + 1) * size
        high_out[...] = high_ref[begin:end, :]
        low_out[...] = low_ref[begin:end, :]


def last_body(levels, owners, mass_ref, q_ref, score_ref):
    mass = mass_ref[0:owners, :]
    for z in range(1, levels):
        mass = mass + mass_ref[z * owners : (z + 1) * owners, :]
    cap = mass.shape[1]
    owner = q_ref[0:1, :]
    rank = q_ref[1:2, :]
    rows = owner.shape[1]
    at_rank = hot(iota((cap, rows), 0) == rank)
    first = mass.astype(jnp.bfloat16)
    rest = mass - first.astype(jnp.float32)
    second, third = halves(rest)
    value = mm(first, at_rank) + mm(second, at_rank) + mm(third, at_rank)
    mine = iota((owners, rows), 0) == owner
    total = jnp.sum(jnp.where(mine, value, 0.0), axis=0, keepdims=True)
    score_ref[...] = jnp.log(total * math.exp(-SHARPNESS)).reshape(rows)


def body(embeddings, cluster_ids, owner_map, source_order):
    rows, width = embeddings.shape
    clusters = owner_map.shape[0]
    levels = lax.axis_size("outer")
    inner = lax.axis_size("inner")
    groups = lax.axis_size("grp")
    owners = levels * inner
    held = clusters // owners
    cap = 2 * rows // owners
    per = cap // CHUNKS
    size = owners * per
    slots = CHUNKS * size
    bf, i32 = jnp.bfloat16, jnp.int32
    dealt = [out((owners, per + extra, width)) for extra in (8, held, 0)]

    first, info = call(
        functools.partial(front_body, owners, per, cap),
        (dealt[0], out((8, rows), i32)),
        embeddings, cluster_ids, owner_map, micros=5,
    )
    back = call(
        functools.partial(back_body, owners, per, CHUNKS, held),
        tuple(dealt[1:]) + (out((8, rows), i32),),
        embeddings, info, source_order, micros=6,
    )
    sends = (first,) + tuple(back[: CHUNKS - 1])
    q_info = back[CHUNKS - 1]
    tile = size // TILES
    strip = per // TILES
    blocks = slots // tile

    got, mine = [], []
    for k in range(CHUNKS):
        send = sends[k] if k == 0 else lax.optimization_barrier((sends[k], mine[-1]))[0]
        got.append(lax.all_to_all(send, PLANE, 0, 0, tiled=True))
        mine.append(got[k][:, :per, :].reshape(size, width))
    own_ids = got[0][:, per, :cap].reshape(owners, cap)
    piece = jnp.sum(got[1][:, per:, :], axis=0)

    level = lax.axis_index("outer")
    down = lax.axis_index("inner") % 2
    seat = jnp.where(down == 1, levels - 1 - level, level)

    def pairs(moves):
        found = []
        for lane in range(inner):
            for a, b in moves:
                if lane % 2:
                    a, b = levels - 1 - a, levels - 1 - b
                found.append((a * inner + lane, b * inner + lane))
        return found

    top = levels - 1
    moves = []
    for s in range(1, top + 1):
        moves.append([(a, a + 1) for a in range(s - 1, top) if not (s == 1 and a == top - 1)])
    back_move = [(top, top - 1)]

    arrived = {}

    def direct(steps):
        return [(a, a + steps) for a in range(top + 1 - steps) if not (steps == 1 and a == top - 1)]

    ids_of = [own_ids]
    for s in range(1, top + 1):
        ids_of.append(lax.ppermute(own_ids, LINE, pairs(direct(s))))
    ids_of.insert(2, lax.ppermute(own_ids, LINE, pairs(back_move)))
    for k in range(CHUNKS):
        value = mine[k]
        for s in range(1, top + 1):
            value = lax.ppermute(value, LINE, pairs(moves[s - 1]))
            arrived[s, k] = value
        arrived["b", k] = lax.ppermute(mine[k], LINE, pairs(back_move))

    def mark(value, through):
        vm = pl.BlockSpec(memory_space=VMEM)
        return pl.pallas_call(
            tick_body, out_shape=out(through.shape), in_specs=[pl.BlockSpec(memory_space=pl.ANY), vm], out_specs=vm
        )(value, through)

    ids_of[0] = mark(arrived[1, 0], own_ids)
    keys_held = len(ids_of)
    ids, flags = call(
        functools.partial(meta_body, owners, CHUNKS),
        (out((keys_held, blocks, 1, tile)), out((8, LANES), i32)),
        *ids_of, micros=3,
    )
    keys = [1, "b"] + list(range(2, top + 1))

    def source_seat(key):
        if key == "b":
            return jnp.where(seat == top - 1, top, -1)
        got = seat >= key
        if key == 1:
            got = got & (seat < top)
        return jnp.where(got, seat - key, -1)

    seats = [seat] + [source_seat(key) for key in keys]
    level_of = jnp.stack([jnp.where(a < 0, -1, jnp.where(down == 1, top - a, a)) for a in seats]).astype(i32)
    part = jnp.zeros((levels, slots), jnp.float32)

    def gram(part, items, held, micros):
        own = items[0][0] == "own"
        visitors = [mine[k] if key == "own" else arrived[key, k] for key, k in items]
        at = tuple((0 if key == "own" else 1 + keys.index(key), k) for key, k in items)
        count = len(items)
        vm = pl.BlockSpec(memory_space=VMEM)
        any_ = pl.BlockSpec(memory_space=pl.ANY)
        own_out = ()
        if own:
            own_out = (out((count * size, width), bf),) * 2 + ((out((slots, LANES)),) if not held else ())
        scratch = [
            VMEM((slots, LANES), jnp.float32),
            VMEM((count, size, width), jnp.float32),
            VMEM((blocks if own else count * TILES, 8, tile), jnp.float32),
            pltpu.SMEM((6, count * TILES * blocks + 1), i32),
            pltpu.SemaphoreType.DMA((count,)),
            VMEM((slots, width), bf),
            VMEM((slots, width), bf),
            VMEM((slots, LANES), jnp.float32),
        ]
        if not own:
            scratch += [VMEM((count * size, width), bf)] * 2
        scratch += [pltpu.SemaphoreType.DMA((6,))]
        return pl.pallas_call(
            functools.partial(gram_body, owners, at, own, len(held)),
            out_shape=(out((levels, slots)),) + own_out,
            in_specs=[pl.BlockSpec(memory_space=pltpu.SMEM)] * 2 + [any_] * (count + len(held)) + [vm, any_],
            out_specs=(vm,) * (1 + len(own_out)),
            scratch_shapes=scratch,
            cost_estimate=cost(micros),
            name="gram",
        )(level_of, flags, *visitors, *held, ids, part)

    plan = [
        ([("own", k) for k in range(CHUNKS)], 13),
        ([(1, 0), ("b", 0), (2, 0)], 14),
        ([(1, 1), (2, 1)], 11),
        ([("b", 1), (1, 2), (2, 2), (3, 0)], 17),
        ([(3, 1), ("b", 2)], 8),
        ([(3, 2)], 8),
    ]
    held_here = ()
    for items, micros in plan:
        part, *made = gram(part, items, held_here, micros)
        held_here += tuple(made)
    total = None
    for s in range(groups):
        route = [(g * levels + z, ((z + s) % groups) * levels + g) for g in range(groups) for z in range(levels)]
        came = lax.ppermute(piece, ("grp", "outer"), route)
        total = came if total is None else total + came
    centroids = total * lax.rsqrt(jnp.mean(total * total, axis=1, keepdims=True) + 1e-6)
    parts = part.reshape(levels, CHUNKS, TILES, owners, strip).transpose(0, 3, 1, 2, 4).reshape(levels * owners, cap)
    home = lax.all_to_all(parts, BY_LEVEL, 0, 0, tiled=True)
    score = call(functools.partial(last_body, levels, owners), out((rows,)), home, q_info, micros=2)

    return score, centroids


def solution(mesh):
    groups, owned = mesh.shape["grp"], mesh.shape["own"]
    split = Mesh(mesh.devices.reshape(groups, groups, owned // groups), EVERY)
    return jax.shard_map(
        body,
        mesh=split,
        in_specs=(P(EVERY, None), P(EVERY), P(), P(EVERY)),
        out_specs=(P(EVERY), P(LINE, None)),
        check_vma=False,
    )
```
